32 devices in a mesh: group: 2 (over x), row: 8 (over z, y), expert: 2 (over core).
Axes of the slice: x: 2, y: 2, z: 4, core: 2. Of those that a mesh axis runs over, the one named last changes fastest.
Arguments:
- tokens: bfloat16 [2, 128, 128, 1024], P('group', ('row', 'expert')), parts along dimension 0, may hold values from -30 to 30
- ln_first: float32 [1024], replicated, may hold values from 0.5 to 1.5
- spec_first: bfloat16 [2, 8, 128, 128], replicated, may hold values from -0.375 to 0.375
- spec_second: bfloat16 [2, 8, 128, 128], replicated, may hold values from -0.375 to 0.375
- spec_bias: float32 [2, 1024], replicated, may hold values from -3 to 3
- ln_second: float32 [1024], replicated, may hold values from 0.5 to 1.5
- routing: int32 [2, 128, 128, 4], P('group', ('row', 'expert')), parts along dimension 0, may hold values from 0 to 3, as said below
- combine: float32 [2, 128, 128, 4], P('group', ('row', 'expert')), parts along dimension 0, may hold values from 0.1 to 0.6
- up_weight: bfloat16 [8, 1024, 1536], P('row'), may hold values from -0.1875 to 0.1875
- down_weight: bfloat16 [8, 1536, 1024], P('row'), may hold values from -0.109375 to 0.109375
Outputs:
- block_out: bfloat16 [2, 128, 128, 1024], P('group', ('row', 'expert')), parts along dimension 0
The draws below stay inside these ranges and needn't reach their ends.
There are 2 independent parts, one for each index of `group`. The reference program is written for one: setup_inputs(seed, part) draws one part's arguments, and reference() takes and returns one part's arrays. A program takes and returns all parts, laid end to end along the dimension named above; an argument that names none is the same for every part. Nothing has to cross between parts.
Inputs may be any that keep to these rules, and one draw needn't show every extreme that they name: `routing`: each token names 4 different experts, and the 1024 tokens held by each index of row+expert name every expert exactly 1024 times.
All inputs are finite; a program needn't handle non-finite values.
Results may differ from the reference program's by a relative error of at most 0.006.
Values may be sent and summed in bfloat16 or wider, within the bound.
A program may use at most 128 MiB of HBM per device.

```python
import math
import jax
import jax.numpy as jnp
from jax import lax

GRID = 128
D = 1024
FF = 3072
NB = 8
TOPK = 4
GRIDS = 1
TOK_DEV = 1024
EXPERTS = 4


def draw_tokens(key, part):
    key_base, key_row, key_col = jax.random.split(jax.random.fold_in(key, 11), 3)
    full_shape = (GRIDS, GRID, GRID, D)
    base_values = jnp.clip(jax.random.normal(key_base, full_shape, jnp.float32), -5.0, 5.0)
    row_scale = jnp.exp(jax.random.uniform(key_row, (GRIDS, GRID, GRID, 1), jnp.float32, math.log(0.3), math.log(3.0)))
    col_scale = jnp.exp(jax.random.uniform(key_col, (1, 1, 1, D), jnp.float32, math.log(0.5), math.log(2.0)))
    return (base_values * row_scale * col_scale).astype(jnp.bfloat16)


def draw_routing(key, part):
    n_devices = GRIDS * GRID * GRID // TOK_DEV
    rows_local = TOK_DEV // (GRIDS * GRID)
    group_size = EXPERTS // TOPK

    def one_block(block_key):
        sub_keys = jax.random.split(block_key, TOPK + 1)
        expert_order = jax.random.permutation(sub_keys[0], EXPERTS).astype(jnp.int32)
        columns = []
        for position in range(TOPK):
            token_ranks = jax.random.permutation(sub_keys[position + 1], TOK_DEV).astype(jnp.int32)
            columns.append(expert_order[position * group_size + token_ranks % group_size])
        return jnp.stack(columns, axis=1)
    all_blocks = jax.vmap(one_block)(jax.random.split(jax.random.fold_in(key, 7), n_devices))
    all_blocks = all_blocks.reshape(n_devices, GRIDS, rows_local, GRID, TOPK).transpose(1, 0, 2, 3, 4)
    return all_blocks.reshape(GRIDS, GRID, GRID, TOPK).astype(jnp.int32)


def shard_levels(rng, extent, shards, low, top_value):
    level = 1.0
    for dim, blocks in shards:
        heights = jax.random.uniform(jax.random.fold_in(jax.random.fold_in(rng, 6), dim), (blocks,), jnp.float32, low / len(shards), top_value / len(shards))
        level = level * jnp.repeat(jnp.exp(heights), extent[dim] // blocks).reshape((-1,) + (1,) * (len(extent) - 1 - dim))
    return level


def bell_draw(own_key, shape, scale, bound, pieces=(), held_as=jnp.bfloat16):
    result = jax.random.normal(own_key, shape, jnp.float32) * scale
    if len(pieces) > 0:
        result = shard_levels(own_key, shape, pieces, -0.22, 0.18) * result
    return jnp.clip(result, min=-bound, max=bound).astype(held_as)


def setup_inputs(seed: int = 0, part: int = 0) -> dict:
    keys = jax.random.split(jax.random.key(seed), 11)
    part_keys = jax.random.split(jax.random.fold_in(keys[10], part), 11)
    return {
        "tokens": draw_tokens(jax.random.fold_in(jax.random.fold_in(keys[10], part), 71), part),
        "ln_first": jnp.clip(1.0 + 0.1 * jax.random.normal(keys[1], (D,), jnp.float32), 0.5, 1.5),
        "spec_first": bell_draw(keys[2], (2, NB, D // NB, D // NB), (2 * D // NB) ** -0.5, 0.375),
        "spec_second": bell_draw(keys[3], (2, NB, D // NB, D // NB), (2 * D // NB) ** -0.5, 0.375),
        "spec_bias": bell_draw(keys[4], (2, D), 0.5, 3.0, (), jnp.float32),
        "ln_second": jnp.clip(1.0 + 0.1 * jax.random.normal(keys[5], (D,), jnp.float32), 0.5, 1.5),
        "routing": draw_routing(jax.random.fold_in(jax.random.fold_in(keys[10], part), 71), part),
        "combine": jnp.clip(0.1 + 0.5 * jax.random.uniform(part_keys[7], (GRIDS, GRID, GRID, TOPK), jnp.float32) ** shard_levels(part_keys[7], (GRIDS, GRID, GRID, TOPK), ((1, 16),), -0.2, 0.2), 0.1, 0.6),
        "up_weight": bell_draw(keys[8], (2 * EXPERTS, D, FF // 2), D ** -0.5, 0.1875, ((0, 8),)),
        "down_weight": bell_draw(keys[9], (2 * EXPERTS, FF // 2, D), FF ** -0.5, 0.109375, ((0, 8),)),
    }


def twiddle(length):
    counter = jnp.arange(length, dtype=jnp.float32)
    angle = 2.0 * math.pi / length * jnp.mod(jnp.outer(counter, counter), float(length))
    return (jnp.cos(angle), jnp.sin(angle))

def layer_norm(values, gain):
    values = values.astype(jnp.float32)
    center = values - lax.optimization_barrier(jnp.mean(values, axis=-1, keepdims=True))
    spread = lax.optimization_barrier(jnp.mean(center * center, axis=-1, keepdims=True))
    return center * lax.rsqrt(spread + 1e-05) * gain

def product(left, right, form):
    return jnp.einsum(form, left.astype(jnp.float32), right.astype(jnp.float32), precision=lax.Precision.HIGHEST)

def complex_blocks(real_in, imag_in, weight):
    form = 'ghkbi,bio->ghkbo'
    real_out = product(real_in, weight[0], form) - product(imag_in, weight[1], form)
    imag_out = product(real_in, weight[1], form) + product(imag_in, weight[0], form)
    return (real_out, imag_out)

def block_mlp(modes, first, second, bias):
    dims = modes.shape
    nblocks = first.shape[1]
    bwidth = first.shape[2]
    real_part = modes[:, 0].reshape(dims[0], dims[2], dims[3], nblocks, bwidth)
    imag_part = modes[:, 1].reshape(dims[0], dims[2], dims[3], nblocks, bwidth)
    hid_real, hid_imag = complex_blocks(real_part, imag_part, first)
    hid_real = jax.nn.relu(hid_real + bias[0].reshape(nblocks, bwidth)).astype(jnp.bfloat16)
    hid_imag = jax.nn.relu(hid_imag + bias[1].reshape(nblocks, bwidth)).astype(jnp.bfloat16)
    out_real, out_imag = complex_blocks(hid_real, hid_imag, second)
    return jnp.stack([out_real, out_imag], axis=1).reshape(dims).astype(jnp.bfloat16)

def reference(tokens, ln_first, spec_first, spec_second, spec_bias, ln_second, routing, combine, up_weight, down_weight):
    cosine, sine = twiddle(GRID)
    forward_cols = jnp.stack([cosine, -sine], axis=1).astype(jnp.bfloat16)
    forward_rows = jnp.stack([jnp.stack([cosine, sine], axis=1), jnp.stack([-sine, cosine], axis=1)], axis=0).astype(jnp.bfloat16)
    inverse_rows = jnp.stack([jnp.stack([cosine, -sine], axis=1), jnp.stack([sine, cosine], axis=1)], axis=0).astype(jnp.bfloat16)
    inverse_cols = jnp.stack([cosine, -sine], axis=0).astype(jnp.bfloat16)
    normed_first = layer_norm(tokens, ln_first).astype(jnp.bfloat16)
    col_spec = product(normed_first, forward_cols, 'ghwd,wck->gchkd').astype(jnp.bfloat16)
    modes = (product(forward_rows, col_spec, 'amch,gchkd->gamkd') * (1.0 / GRID)).astype(jnp.bfloat16)
    mixed_modes = block_mlp(modes, spec_first, spec_second, spec_bias)
    row_back = product(inverse_rows, mixed_modes, 'amch,gchkd->gamkd').astype(jnp.bfloat16)
    mixing = product(row_back, inverse_cols, 'gchkd,ckw->ghwd') * (1.0 / GRID)
    residual = (tokens.astype(jnp.float32) + mixing).astype(jnp.bfloat16)
    normed = layer_norm(residual, ln_second).astype(jnp.bfloat16).reshape(-1, D)
    flat_route = routing.reshape(-1).astype(jnp.int32)
    weights_flat = combine.reshape(-1)
    order_all = jnp.argsort(flat_route, stable=True).astype(jnp.int32).reshape(EXPERTS, -1)
    up_full = up_weight.reshape(EXPERTS, 2, D, FF // 2).transpose(0, 2, 1, 3).reshape(EXPERTS, D, FF)
    down_full = down_weight.reshape(EXPERTS, FF, D)

    def one_expert(inputs):
        picks, w_up, w_down = inputs
        rows_in = normed[picks // TOPK]
        hidden = jax.nn.gelu(jnp.dot(rows_in, w_up, preferred_element_type=jnp.float32), approximate=True).astype(jnp.bfloat16)
        return jnp.dot(hidden, w_down, preferred_element_type=jnp.float32) * weights_flat[picks][:, None]
    outputs = lax.map(one_expert, (order_all, up_full, down_full))
    total = jnp.zeros(normed.shape, jnp.float32).at[order_all.reshape(-1) // TOPK].add(outputs.reshape(-1, D))
    return (residual.astype(jnp.float32) + total.reshape(residual.shape)).astype(jnp.bfloat16)
```

```python
import math

import jax
import jax.numpy as jnp
import numpy as np
from jax import lax
from jax.experimental import pallas as pl
from jax.experimental.pallas import tpu as pltpu
from jax.sharding import PartitionSpec as P


def from_partner(value, axis, stride):
    mask = 2**stride
    pairs = [(source, source ^ mask) for source in range(lax.axis_size(axis))]
    return lax.ppermute(value, axis, pairs)


def twiddle(length):
    counter = jnp.arange(length, dtype=jnp.float32)
    angle = 2.0 * math.pi / length * jnp.mod(jnp.outer(counter, counter), float(length))
    return (jnp.cos(angle), jnp.sin(angle))


def layer_norm(values, gain):
    values = values.astype(jnp.float32)
    center = values - jnp.mean(values, axis=-1, keepdims=True)
    spread = jnp.mean(center * center, axis=-1, keepdims=True)
    return center * lax.rsqrt(spread + 1e-05) * gain


def product(left, right, form):
    return jnp.einsum(form, left, right, preferred_element_type=jnp.float32)


def complex_blocks(real_in, imag_in, weight):
    form = "ghkbi,bio->ghkbo"
    real_out = product(real_in, weight[0], form) - product(imag_in, weight[1], form)
    imag_out = product(real_in, weight[1], form) + product(imag_in, weight[0], form)
    return (real_out, imag_out)


def block_mlp(modes, first, second, bias):
    dims = modes.shape
    nblocks = first.shape[1]
    bwidth = first.shape[2]
    real_part = modes[:, 0].reshape(dims[0], dims[2], dims[3], nblocks, bwidth)
    imag_part = modes[:, 1].reshape(dims[0], dims[2], dims[3], nblocks, bwidth)
    hid_real, hid_imag = complex_blocks(real_part, imag_part, first)
    hid_real = jax.nn.relu(hid_real + bias[0].reshape(nblocks, bwidth)).astype(jnp.bfloat16)
    hid_imag = jax.nn.relu(hid_imag + bias[1].reshape(nblocks, bwidth)).astype(jnp.bfloat16)
    out_real, out_imag = complex_blocks(hid_real, hid_imag, second)
    return jnp.stack([out_real, out_imag], axis=1).reshape(dims).astype(jnp.bfloat16)


def run_expert(arrived, up_full, down_full):
    in_shape = arrived.shape
    width = arrived.shape[2]
    hidden = jax.nn.gelu(
        jnp.dot(arrived.reshape(-1, width), up_full, preferred_element_type=jnp.float32),
        approximate=True,
    ).astype(jnp.bfloat16)
    partial_out = jnp.dot(hidden, down_full, preferred_element_type=jnp.float32).reshape(
        in_shape[0], in_shape[1], width
    )
    return lax.all_to_all(
        partial_out.astype(jnp.bfloat16), "row", split_axis=0, concat_axis=0, tiled=True
    ).astype(partial_out.dtype)


def per_device(
    tokens,
    ln_first,
    spec_first,
    spec_second,
    spec_bias,
    ln_second,
    routing,
    combine,
    up_weight,
    down_weight,
):
    grid_len = tokens.shape[2]
    width = tokens.shape[3]
    cosine, sine = twiddle(grid_len)
    forward_cols = jnp.stack([cosine, -sine], axis=1).astype(jnp.bfloat16)
    forward_rows = jnp.stack(
        [jnp.stack([cosine, sine], axis=1), jnp.stack([-sine, cosine], axis=1)], axis=0
    ).astype(jnp.bfloat16)
    inverse_rows = jnp.stack(
        [jnp.stack([cosine, -sine], axis=1), jnp.stack([sine, cosine], axis=1)], axis=0
    ).astype(jnp.bfloat16)
    inverse_cols = jnp.stack([cosine, -sine], axis=0).astype(jnp.bfloat16)
    normed_first = layer_norm(tokens, ln_first).astype(jnp.bfloat16)
    col_spec = product(normed_first, forward_cols, "ghwd,wck->gchkd").astype(jnp.bfloat16)
    by_column = lax.all_to_all(col_spec, ("row", "expert"), split_axis=3, concat_axis=2, tiled=True)
    modes = (product(forward_rows, by_column, "amch,gchkd->gamkd") * (1.0 / grid_len)).astype(
        jnp.bfloat16
    )
    mixed_modes = block_mlp(modes, spec_first, spec_second, spec_bias)
    row_back = product(inverse_rows, mixed_modes, "amch,gchkd->gamkd").astype(jnp.bfloat16)
    by_row = lax.all_to_all(row_back, ("row", "expert"), split_axis=2, concat_axis=3, tiled=True)
    mixing = product(by_row, inverse_cols, "gchkd,ckw->ghwd") * (1.0 / grid_len)
    residual = (tokens.astype(jnp.float32) + mixing).astype(jnp.bfloat16)
    normed = layer_norm(residual, ln_second).astype(jnp.bfloat16).reshape(-1, width)
    n_tokens = normed.shape[0]
    top_count = routing.shape[-1]
    experts = lax.axis_size("row") // 2
    capacity = n_tokens * top_count // experts
    flat_route = routing.reshape(-1)
    one_hot = (flat_route[:, None] == jnp.arange(experts, dtype=jnp.int32)[None, :]).astype(
        jnp.int32
    )
    earlier = jnp.cumsum(one_hot, axis=0) - one_hot
    slot_index = flat_route * capacity + jnp.sum(earlier * one_hot, axis=1)
    token_of = jnp.arange(n_tokens * top_count, dtype=jnp.int32) // top_count
    source_row = jnp.zeros((experts * capacity,), jnp.int32).at[slot_index].set(token_of)
    send_rows = normed[source_row].reshape(experts, capacity, width)
    partner_up, partner_down = from_partner((up_weight, down_weight), "row", 0)
    up_full = jnp.concatenate([up_weight[0], partner_up[0]], axis=1)
    down_full = jnp.concatenate([down_weight[0], partner_down[0]], axis=0)
    outgoing = send_rows.reshape(experts * 2, capacity // 2, width)
    returned = run_expert(
        lax.all_to_all(outgoing, "row", split_axis=0, concat_axis=0, tiled=True), up_full, down_full
    )
    results = returned.reshape(experts, capacity, width)
    gathered = results.reshape(-1, width)[slot_index].reshape(n_tokens, top_count, width)
    moe_out = jnp.sum(gathered * combine.reshape(n_tokens, top_count, 1), axis=1)
    final = residual.reshape(-1, width).astype(jnp.float32) + moe_out
    return final.reshape(tokens.shape).astype(jnp.bfloat16)


LANES = 256
PARTS = 2


def rank_tables(length, ranks):
    counter = np.arange(length)
    angle = 2.0 * np.pi / length * np.mod(np.outer(counter, counter), length)
    cosine, sine = np.cos(angle), np.sin(angle)
    half = length // 2
    second = -sine[:half]
    second[0] = cosine[half]
    packed = np.stack([cosine[:half], second])
    packed = packed.reshape(2, ranks, half // ranks, length).transpose(1, 0, 2, 3)
    packed = packed.reshape(length, length)
    tables = np.stack([cosine, sine, packed, packed.T])
    return jnp.asarray(tables, jnp.float32).astype(jnp.bfloat16)


def pick(index, values):
    out = values[-1]
    for place, value in enumerate(values[:-1]):
        out = jnp.where(index == place, value, out)
    return out


def norm_rows(values, gain):
    center = values - jnp.mean(values, axis=-1, keepdims=True)
    spread = jnp.mean(center * center, axis=-1, keepdims=True)
    return center * lax.rsqrt(spread + 1e-05) * gain


def block_kernel(
    sizes,
    tokens_ref,
    ln_first_ref,
    ln_second_ref,
    tables_ref,
    first_ref,
    second_ref,
    bias_ref,
    gates_ref,
    up_hbm,
    down_hbm,
    out_ref,
    columns,
    columns_t,
    rows_d,
    rows_dt,
    spec_send,
    spec_recv,
    back_send,
    back_recv,
    resid,
    acts,
    gates,
    total,
    ups,
    downs,
    a2a_send,
    a2a_recv,
    z_send,
    z_recv,
    x_send,
    x_recv,
    c_send,
    c_recv,
    swap_send,
    swap_recv,
    local_sem,
):
    groups, rows_axis, cores = sizes
    planes = rows_axis // 2
    ranks = rows_axis * cores
    group, row, core = lax.axis_index("group"), lax.axis_index("row"), lax.axis_index("expert")
    plane = row // 2
    me = row * cores + core
    n_tokens, width = tokens_ref.shape
    lanes = spec_send.shape[2]
    chunks = width // lanes
    grid_len = tables_ref.shape[1]
    slots = grid_len // 2 // ranks
    block_rows = n_tokens // ranks
    bwidth = first_ref.shape[2]
    per_step = lanes // bwidth
    scale = 1.0 / grid_len
    hidden = ups.shape[2]
    step = n_tokens // 2
    bf16 = jnp.bfloat16

    def device(g, r, c):
        return {"group": g, "row": r, "expert": c}

    def remote(source, target, send, recv, where):
        return pltpu.make_async_remote_copy(
            src_ref=source,
            dst_ref=target,
            send_sem=send,
            recv_sem=recv,
            device_id=where,
            device_id_type=pl.DeviceIdType.MESH,
        )

    barrier = pltpu.get_barrier_semaphore()
    for offset in range(1, ranks):
        other = lax.rem(me + offset, ranks)
        pl.semaphore_signal(
            barrier,
            inc=1,
            device_id=device(group, other // cores, other % cores),
            device_id_type=pl.DeviceIdType.MESH,
        )
    pl.semaphore_signal(
        barrier,
        inc=1,
        device_id=device(1 - group, row, core),
        device_id_type=pl.DeviceIdType.MESH,
    )
    pl.semaphore_wait(barrier, ranks)

    shares = groups * cores
    share = group * cores + core
    side_share = (1 - group) * cores + core
    pieces = 2 * PARTS

    def view(ref, base, quarter, piece):
        size = ref.shape[1] // shares // PARTS
        start = (quarter * PARTS + piece % PARTS) * size
        return ref.at[base, pl.ds(pl.multiple_of(start, 32), size), :]

    def held(expert, quarter, piece):
        return view(ups if piece < PARTS else downs, expert, quarter, piece)

    def source(piece):
        return view(up_hbm if piece < PARTS else down_hbm, 0, share, piece)

    def plane_copy(expert, piece, src, way, target_plane):
        return remote(
            src,
            held(expert, share, piece),
            z_send.at[way, expert, piece],
            z_recv.at[expert, piece],
            device(group, 2 * target_plane + row % 2, core),
        )

    def side_copy(expert, piece):
        return remote(
            held(expert, share, piece),
            held(expert, share, piece),
            x_send.at[expert, piece],
            x_recv.at[expert, piece],
            device(1 - group, row, core),
        )

    def core_copy(expert, piece, which):
        part = held(expert, side_share if which else share, piece)
        return remote(
            part,
            part,
            c_send.at[which, expert, piece],
            c_recv.at[which, expert, piece],
            device(group, row, 1 - core),
        )

    near = plane + 1 - 2 * (plane % 2)
    far = plane - 1 + 2 * (plane % 2)
    inner = (far >= 0) & (far < planes)
    safe_far = jnp.clip(far, 0, planes - 1)
    arrivals = [[2 * (p // 2) + 1 - p % 2] for p in range(planes)]
    for p in range(planes):
        arrivals[p] += sorted((q for q in range(planes) if q // 2 != p // 2), key=lambda q: abs(q - p))
    expert_at = [plane] + [pick(plane, [a[t] for a in arrivals]) for t in range(planes - 1)]

    def own_copies(piece):
        return plane_copy(plane, piece, source(piece), 0, near)

    def far_own(piece):
        return plane_copy(plane, piece, source(piece), 1, safe_far)

    def forward(t, piece):
        expert = expert_at[t]
        target = safe_far if t == 1 else near
        return plane_copy(expert, piece, held(expert, share, piece), 0, target)

    def relay(t, piece, stage):
        expert = expert_at[t]
        if stage == 0:
            plane_copy(expert, piece, held(expert, share, piece), 0, near).wait_recv()
            if t > 1:

                @pl.when(inner)
                def _():
                    forward(t, piece).start()

            side_copy(expert, piece).start()
            core_copy(expert, piece, 0).start()
        else:
            side_copy(expert, piece).wait_recv()
            core_copy(expert, piece, 1).start()

    def ready(t):
        for piece in range(pieces):
            for which in range(2):
                core_copy(expert_at[t], piece, which).wait_recv()

    half = row % 2
    partner = device(group, row + 1 - 2 * half, core)
    gate_copy = remote(gates_ref, gates.at[1], swap_send.at[0], swap_recv.at[0], partner)
    gate_copy.start()
    for piece in range(PARTS):
        own_copies(piece).start()
    up_local = pltpu.make_async_copy(up_hbm.at[0], ups.at[plane], local_sem.at[0])
    down_local = pltpu.make_async_copy(down_hbm.at[0], downs.at[plane], local_sem.at[1])
    up_local.start()
    down_local.start()

    @pl.loop(0, n_tokens // grid_len)
    def _(index):
        rows = pl.ds(pl.multiple_of(index * grid_len, grid_len), grid_len)
        acts[0, rows, :] = norm_rows(tokens_ref[rows, :].astype(jnp.float32), ln_first_ref[...]).astype(
            bf16
        )

    my_rows = n_tokens // grid_len
    spread = jnp.broadcast_to(
        tables_ref[2].astype(jnp.float32)[:, None, :], (grid_len, my_rows, grid_len)
    ).reshape(n_tokens, grid_len)
    place = lax.broadcasted_iota(jnp.int32, (n_tokens, grid_len), 0) % my_rows
    for index in range(my_rows):
        columns[:, index * grid_len : (index + 1) * grid_len] = jnp.where(
            place == index, spread, 0.0
        ).astype(bf16)

    order = sorted(range(1, ranks), key=lambda offset: abs(offset - ranks // 2))

    def exchange(stage, send_ref, recv_ref, chunk, offset):
        other = lax.rem(me + offset, ranks)
        return remote(
            send_ref.at[chunk, pl.ds(pl.multiple_of(other * block_rows, block_rows), block_rows), :],
            recv_ref.at[chunk, pl.ds(pl.multiple_of(me * block_rows, block_rows), block_rows), :],
            a2a_send.at[stage, chunk, offset],
            a2a_recv.at[stage, chunk, offset],
            device(group, other // cores, other % cores),
        )

    def arrived(stage, send_ref, recv_ref, chunk, offset):
        other = lax.rem(me + ranks - offset, ranks)
        return remote(
            send_ref.at[chunk, pl.ds(pl.multiple_of(me * block_rows, block_rows), block_rows), :],
            recv_ref.at[chunk, pl.ds(pl.multiple_of(other * block_rows, block_rows), block_rows), :],
            a2a_send.at[stage, chunk, offset],
            a2a_recv.at[stage, chunk, offset],
            device(group, other // cores, other % cores),
        )

    def keep_own(send_ref, recv_ref, chunk):
        mine = pl.ds(pl.multiple_of(me * block_rows, block_rows), block_rows)
        recv_ref[chunk, mine, :] = send_ref[chunk, mine, :]

    @pl.loop(0, chunks)
    def _(chunk):
        cut = pl.ds(pl.multiple_of(chunk * lanes, lanes), lanes)
        spec_send[chunk] = jnp.dot(
            columns[...], acts[0, :, cut], preferred_element_type=jnp.float32
        ).astype(bf16)
        for offset in order:
            exchange(0, spec_send, spec_recv, chunk, offset).start()
        keep_own(spec_send, spec_recv, chunk)

    picker = lax.broadcasted_iota(jnp.int32, (grid_len, n_tokens), 1) // my_rows
    picker = picker == lax.broadcasted_iota(jnp.int32, (grid_len, n_tokens), 0)
    picker = jnp.where(picker, 1.0, 0.0).astype(bf16)
    spread_t = jnp.dot(tables_ref[3], picker, preferred_element_type=jnp.float32)
    place_t = lax.broadcasted_iota(jnp.int32, (grid_len, n_tokens), 1) % my_rows
    for index in range(my_rows):
        columns_t[index * grid_len : (index + 1) * grid_len, :] = jnp.where(
            place_t == index, spread_t, 0.0
        ).astype(bf16)
    cosine, sine = tables_ref[0], tables_ref[1]
    none = jnp.zeros_like(cosine)

    def fill(slot, grid):
        for index, (left, right) in enumerate(grid):
            cut = slice(index * grid_len, (index + 1) * grid_len)
            rows_d[slot, cut, :grid_len] = left
            rows_d[slot, cut, grid_len:] = right
            rows_dt[slot, :grid_len, cut] = left
            rows_dt[slot, grid_len:, cut] = right

    usual = [(cosine, sine), (cosine, -sine), (-sine, cosine), (-sine, -cosine)]
    fill(0, usual)

    @pl.when(me == 0)
    def _():
        fill(1, [(cosine, none), (none, cosine), (-sine, none), (none, -sine)])

    @pl.when(me != 0)
    def _():
        fill(1, usual)

    gates[0] = gates_ref[...]
    total[...] = jnp.zeros_like(total)

    def square(ref, block):
        real, imag = ref[0, block], ref[1, block]
        top = jnp.concatenate([real, imag], axis=1)
        return jnp.concatenate([top, jnp.concatenate([-imag, real], axis=1)], axis=0)

    def mix(chunk):
        values = spec_recv[chunk].astype(jnp.float32).reshape(ranks, 2 * slots, my_rows, lanes)
        real_parts, imag_parts = [], []
        for slot in range(slots):
            pair = jnp.concatenate(
                [
                    values[:, slot].reshape(grid_len, lanes),
                    values[:, slots + slot].reshape(grid_len, lanes),
                ],
                axis=0,
            ).astype(bf16)
            matrix = rows_d[1 if slot == 0 else 0]
            modes = jnp.dot(matrix, pair, preferred_element_type=jnp.float32) * scale
            modes = modes.astype(bf16)
            real_parts.append(modes[: 2 * grid_len])
            imag_parts.append(modes[2 * grid_len :])
        real = jnp.concatenate(real_parts, axis=0)
        imag = jnp.concatenate(imag_parts, axis=0)
        mixed_real, mixed_imag = [], []
        for index in range(per_step):
            block = chunk * per_step + index
            cut = slice(index * bwidth, (index + 1) * bwidth)
            both = jnp.concatenate([real[:, cut], imag[:, cut]], axis=1)
            place = pl.ds(pl.multiple_of(block * bwidth, bwidth), bwidth)
            bias = jnp.concatenate([bias_ref[0:1, place], bias_ref[1:2, place]], axis=1)
            hid = jnp.dot(both, square(first_ref, block), preferred_element_type=jnp.float32) + bias
            hid = jnp.maximum(hid, 0.0).astype(bf16)
            mixed = jnp.dot(hid, square(second_ref, block), preferred_element_type=jnp.float32)
            mixed = mixed.astype(bf16)
            mixed_real.append(mixed[:, :bwidth])
            mixed_imag.append(mixed[:, bwidth:])
        real = jnp.concatenate(mixed_real, axis=1)
        imag = jnp.concatenate(mixed_imag, axis=1)
        back_real, back_imag = [], []
        for slot in range(slots):
            cut = slice(slot * 2 * grid_len, (slot + 1) * 2 * grid_len)
            column = jnp.concatenate([real[cut], imag[cut]], axis=0)
            matrix = rows_dt[1 if slot == 0 else 0]
            back = jnp.dot(matrix, column, preferred_element_type=jnp.float32)
            back_real.append(back[:grid_len].reshape(ranks, my_rows, lanes))
            back_imag.append(back[grid_len:].reshape(ranks, my_rows, lanes))
        out = jnp.stack(back_real + back_imag, axis=1).reshape(n_tokens, lanes)
        back_send[chunk] = out.astype(bf16)

    @pl.loop(0, chunks)
    def _(chunk):
        @pl.when(chunk == 1)
        def _():
            for piece in range(PARTS):
                relay(1, piece, 0)

        @pl.when(chunk == 2)
        def _():
            for piece in range(PARTS):
                relay(1, piece, 1)

        for offset in order:
            arrived(0, spec_send, spec_recv, chunk, offset).wait_recv()
        mix(chunk)
        for offset in order:
            exchange(1, back_send, back_recv, chunk, offset).start()
        keep_own(back_send, back_recv, chunk)

        @pl.when(chunk == 0)
        def _():
            for piece in range(PARTS, pieces):
                own_copies(piece).start()

    @pl.when(inner)
    def _():
        for piece in range(pieces):
            far_own(piece).start()
        for piece in range(PARTS):
            forward(1, piece).start()

    @pl.loop(0, chunks)
    def _(chunk):
        @pl.when(chunk == 2)
        def _():
            for piece in range(PARTS, pieces):
                relay(1, piece, 0)

            @pl.when(inner)
            def _():
                for piece in range(PARTS, pieces):
                    forward(1, piece).start()

        for offset in order:
            arrived(1, back_send, back_recv, chunk, offset).wait_recv()
        cut = pl.ds(pl.multiple_of(chunk * lanes, lanes), lanes)
        mixing = jnp.dot(columns_t[...], back_recv[chunk], preferred_element_type=jnp.float32) * scale
        resid[:, cut] = (tokens_ref[:, cut].astype(jnp.float32) + mixing).astype(bf16)

    def swap_copy(block):
        rows = pl.ds(block * step, step)
        return remote(
            acts.at[0, rows, :],
            acts.at[1, rows, :],
            swap_send.at[1 + block],
            swap_recv.at[1 + block],
            partner,
        )

    def return_copy(block):
        rows = pl.ds(pl.multiple_of(block * step, step), step)
        return remote(
            spec_send.at[:, rows, :],
            spec_recv.at[:, rows, :],
            swap_send.at[3 + block],
            swap_recv.at[3 + block],
            partner,
        )

    for block in range(2):

        @pl.loop(0, my_rows // 2)
        def _(index):
            start = block * step + index * grid_len
            rows = pl.ds(pl.multiple_of(start, grid_len), grid_len)
            acts[0, rows, :] = norm_rows(
                resid[rows, :].astype(jnp.float32), ln_second_ref[...]
            ).astype(bf16)

        swap_copy(block).start()

    @pl.loop(0, chunks)
    def _(chunk):
        for offset in order:
            exchange(0, spec_send, spec_recv, chunk, offset).wait_send()

    plan = [(0, 0, 0), (0, 1, 0), (0, 0, 1), (0, 1, 1)]
    plan += [(1, 0, 0), (1, 0, 1), (1, 1, 0), (1, 1, 1)]
    plan += [(1, 0, 2), (1, 1, 2), (0, 0, 2), (0, 1, 2)]
    plan += [(1, 0, 3), (1, 1, 3), (0, 0, 3), (0, 1, 3)]
    relays = {}

    def at(place_inner, place_outer, t, piece, stage):
        relays[(t, piece, stage)] = jnp.where(inner, place_inner, place_outer)

    for piece in range(pieces):
        share_of = (piece * 4) // pieces
        at((2, 4, 5, 7)[share_of], (4, 5, 7, 8)[share_of], 2, piece, 0)
        at((4, 6, 7, 8)[share_of], (6, 7, 8, 8)[share_of], 2, piece, 1)
        at((8, 9, 11, 12)[share_of], (9, 11, 12, 12)[share_of], 3, piece, 0)
        at((10, 11, 12, 12)[share_of], (11, 12, 12, 12)[share_of], 3, piece, 1)

    def lift(who, rows, expert, cut):
        return jnp.dot(
            acts[who, rows, :], ups[expert, :, cut], preferred_element_type=jnp.float32
        )

    @pl.loop(0, len(plan))
    def _(item):
        who = pick(item, [p[0] for p in plan])
        block = pick(item, [p[1] for p in plan])
        turn = pick(item, [p[2] for p in plan])

        @pl.when(item == 0)
        def _():
            up_local.wait()
            down_local.wait()
            for piece in range(PARTS, pieces):
                relay(1, piece, 1)

        for (t, piece, stage), place in sorted(relays.items(), key=lambda r: (r[0][0], r[0][2], r[0][1])):

            @pl.when(item == place)
            def _():
                relay(t, piece, stage)

        for t, place in ((1, 2), (2, 8), (3, 12)):

            @pl.when(item == place)
            def _():
                ready(t)

        for index, place in ((0, 4), (1, 6)):

            @pl.when(item == place)
            def _():
                swap_copy(index).wait_recv()

        @pl.when(item == 4)
        def _():
            gate_copy.wait_recv()

        expert = pick(turn, expert_at)
        rows = pl.ds(pl.multiple_of(block * step, step), step)
        wide = 512 if hidden % 512 == 0 else hidden
        cuts = [pl.ds(start, wide) for start in range(0, hidden, wide)]
        out, ahead = None, lift(who, rows, expert, cuts[0])
        for index, cut in enumerate(cuts):
            raw = ahead
            if index + 1 < len(cuts):
                ahead = lift(who, rows, expert, cuts[index + 1])
            active = jax.nn.gelu(raw, approximate=True).astype(bf16)
            part = jnp.dot(active, downs[expert, cut, :], preferred_element_type=jnp.float32)
            out = part if out is None else out + part
        lane = lax.broadcasted_iota(jnp.int32, (step, gates.shape[2]), 1)
        gate = jnp.sum(jnp.where(lane == expert, gates[who, rows, :], 0.0), axis=1, keepdims=True)
        total[who, rows, :] = total[who, rows, :] + gate * out

        @pl.when((who == 1) & (turn == planes - 1))
        def _():
            for chunk in range(chunks):
                cut = slice(chunk * lanes, (chunk + 1) * lanes)
                spec_send[chunk, rows, :] = total[1, rows, cut].astype(bf16)
            return_copy(block).start()

    for block in range(2):
        return_copy(block).wait_recv()
        rows = pl.ds(block * step, step)
        for chunk in range(chunks):
            cut = slice(chunk * lanes, (chunk + 1) * lanes)
            final = resid[rows, cut].astype(jnp.float32) + total[0, rows, cut]
            final = final + spec_recv[chunk, rows, :].astype(jnp.float32)
            out_ref[rows, cut] = final.astype(bf16)

    for block in range(2):
        swap_copy(block).wait_send()
        return_copy(block).wait_send()
    gate_copy.wait_send()

    @pl.loop(0, chunks)
    def _(chunk):
        for offset in order:
            exchange(1, back_send, back_recv, chunk, offset).wait_send()

    for piece in range(pieces):
        own_copies(piece).wait_send()
        for t in range(1, planes):
            side_copy(expert_at[t], piece).wait_send()
            for which in range(2):
                core_copy(expert_at[t], piece, which).wait_send()

    @pl.when(inner)
    def _():
        for piece in range(pieces):
            far_own(piece).wait_send()
            for t in range(1, planes):
                forward(t, piece).wait_send()


def per_device_fused(
    sizes,
    tokens,
    ln_first,
    spec_first,
    spec_second,
    spec_bias,
    ln_second,
    routing,
    combine,
    up_weight,
    down_weight,
):
    groups, rows_axis, cores = sizes
    ranks, planes = rows_axis * cores, rows_axis // 2
    _, my_rows, grid_len, width = tokens.shape
    n_tokens = my_rows * grid_len
    lanes = LANES
    chunks = width // lanes
    route = routing.reshape(n_tokens, -1)
    weight = combine.reshape(n_tokens, -1)
    spot = jnp.arange(128, dtype=jnp.int32)
    gates = jnp.zeros((n_tokens, 128), jnp.float32)
    for k in range(route.shape[1]):
        gates = gates + jnp.where(route[:, k : k + 1] == spot[None, :], weight[:, k : k + 1], 0.0)
    hidden = up_weight.shape[2]
    bf16 = jnp.bfloat16
    pieces = 2 * PARTS
    vmem = pl.BlockSpec(memory_space=pltpu.VMEM)
    hbm = pl.BlockSpec(memory_space=pl.ANY)
    dma = pltpu.SemaphoreType.DMA
    out = pl.pallas_call(
        lambda *refs: block_kernel(sizes, *refs),
        in_specs=[vmem] * 8 + [hbm] * 2,
        out_specs=vmem,
        out_shape=jax.ShapeDtypeStruct((n_tokens, width), bf16),
        scratch_shapes=[
            pltpu.VMEM((n_tokens, n_tokens), bf16),
            pltpu.VMEM((n_tokens, n_tokens), bf16),
            pltpu.VMEM((2, 4 * grid_len, 2 * grid_len), bf16),
            pltpu.VMEM((2, 2 * grid_len, 4 * grid_len), bf16),
            pltpu.VMEM((chunks, n_tokens, lanes), bf16),
            pltpu.VMEM((chunks, n_tokens, lanes), bf16),
            pltpu.VMEM((chunks, n_tokens, lanes), bf16),
            pltpu.VMEM((chunks, n_tokens, lanes), bf16),
            pltpu.VMEM((n_tokens, width), bf16),
            pltpu.VMEM((2, n_tokens, width), bf16),
            pltpu.VMEM((2, n_tokens, 128), jnp.float32),
            pltpu.VMEM((2, n_tokens, width), jnp.float32),
            pltpu.VMEM((planes,) + up_weight.shape[1:], bf16),
            pltpu.VMEM((planes,) + down_weight.shape[1:], bf16),
            dma((2, chunks, ranks)),
            dma((2, chunks, ranks)),
            dma((2, planes, pieces)),
            dma((planes, pieces)),
            dma((planes, pieces)),
            dma((planes, pieces)),
            dma((2, planes, pieces)),
            dma((2, planes, pieces)),
            dma((5,)),
            dma((5,)),
            dma((2,)),
        ],
        compiler_params=pltpu.CompilerParams(
            collective_id=0, has_side_effects=True, vmem_limit_bytes=67043328
        ),
        name="block",
    )(
        tokens.reshape(n_tokens, width),
        ln_first.reshape(1, width),
        ln_second.reshape(1, width),
        rank_tables(grid_len, ranks),
        spec_first,
        spec_second,
        spec_bias,
        gates,
        up_weight,
        down_weight,
    )
    return out.reshape(tokens.shape)


def solution(mesh):
    shape = mesh.shape
    group, row, expert = shape["group"], shape["row"], shape["expert"]
    cells = P("group", ("row", "expert"), None, None)
    weights = P("row", None, None)
    ins = (cells, P(), P(), P(), P(), P(), cells, cells, weights, weights)

    def run(*args):
        tokens, first, routing = args[0], args[2], args[6]
        ranks, planes = row * expert, row // 2
        fused = group == 2 and expert == 2 and planes == 4 and routing.shape[-1] == planes
        fused = fused and tokens.shape[0] == group and tokens.shape[1] == 8 * ranks
        fused = fused and (tokens.shape[2] // 2) % ranks == 0 and tokens.shape[2] == 128
        fused = fused and tokens.shape[3] % LANES == 0 and LANES % first.shape[2] == 0
        fused = fused and args[8].shape[1] % 256 == 0 and args[9].shape[1] % 256 == 0
        if fused:
            body = lambda *blocks: per_device_fused((group, row, expert), *blocks)
        else:
            body = per_device
        call = jax.shard_map(body, mesh=mesh, in_specs=ins, out_specs=cells, check_vma=False)
        return call(*args)

    return run
```

```python
import math

import jax
import jax.numpy as jnp
import numpy as np
from jax import lax
from jax.experimental import pallas as pl
from jax.experimental.pallas import tpu as pltpu
from jax.sharding import PartitionSpec as P


def from_partner(value, axis, stride):
    mask = 2**stride
    pairs = [(source, source ^ mask) for source in range(lax.axis_size(axis))]
    return lax.ppermute(value, axis, pairs)


def twiddle(length):
    counter = jnp.arange(length, dtype=jnp.float32)
    angle = 2.0 * math.pi / length * jnp.mod(jnp.outer(counter, counter), float(length))
    return (jnp.cos(angle), jnp.sin(angle))


def layer_norm(values, gain):
    values = values.astype(jnp.float32)
    center = values - jnp.mean(values, axis=-1, keepdims=True)
    spread = jnp.mean(center * center, axis=-1, keepdims=True)
    return center * lax.rsqrt(spread + 1e-05) * gain


def product(left, right, form):
    return jnp.einsum(form, left, right, preferred_element_type=jnp.float32)


def complex_blocks(real_in, imag_in, weight):
    form = "ghkbi,bio->ghkbo"
    real_out = product(real_in, weight[0], form) - product(imag_in, weight[1], form)
    imag_out = product(real_in, weight[1], form) + product(imag_in, weight[0], form)
    return (real_out, imag_out)


def block_mlp(modes, first, second, bias):
    dims = modes.shape
    nblocks = first.shape[1]
    bwidth = first.shape[2]
    real_part = modes[:, 0].reshape(dims[0], dims[2], dims[3], nblocks, bwidth)
    imag_part = modes[:, 1].reshape(dims[0], dims[2], dims[3], nblocks, bwidth)
    hid_real, hid_imag = complex_blocks(real_part, imag_part, first)
    hid_real = jax.nn.relu(hid_real + bias[0].reshape(nblocks, bwidth)).astype(jnp.bfloat16)
    hid_imag = jax.nn.relu(hid_imag + bias[1].reshape(nblocks, bwidth)).astype(jnp.bfloat16)
    out_real, out_imag = complex_blocks(hid_real, hid_imag, second)
    return jnp.stack([out_real, out_imag], axis=1).reshape(dims).astype(jnp.bfloat16)


def run_expert(arrived, up_full, down_full):
    in_shape = arrived.shape
    width = arrived.shape[2]
    hidden = jax.nn.gelu(
        jnp.dot(arrived.reshape(-1, width), up_full, preferred_element_type=jnp.float32),
        approximate=True,
    ).astype(jnp.bfloat16)
    partial_out = jnp.dot(hidden, down_full, preferred_element_type=jnp.float32).reshape(
        in_shape[0], in_shape[1], width
    )
    return lax.all_to_all(
        partial_out.astype(jnp.bfloat16), "row", split_axis=0, concat_axis=0, tiled=True
    ).astype(partial_out.dtype)


def per_device(
    tokens,
    ln_first,
    spec_first,
    spec_second,
    spec_bias,
    ln_second,
    routing,
    combine,
    up_weight,
    down_weight,
):
    grid_len = tokens.shape[2]
    width = tokens.shape[3]
    cosine, sine = twiddle(grid_len)
    forward_cols = jnp.stack([cosine, -sine], axis=1).astype(jnp.bfloat16)
    forward_rows = jnp.stack(
        [jnp.stack([cosine, sine], axis=1), jnp.stack([-sine, cosine], axis=1)], axis=0
    ).astype(jnp.bfloat16)
    inverse_rows = jnp.stack(
        [jnp.stack([cosine, -sine], axis=1), jnp.stack([sine, cosine], axis=1)], axis=0
    ).astype(jnp.bfloat16)
    inverse_cols = jnp.stack([cosine, -sine], axis=0).astype(jnp.bfloat16)
    normed_first = layer_norm(tokens, ln_first).astype(jnp.bfloat16)
    col_spec = product(normed_first, forward_cols, "ghwd,wck->gchkd").astype(jnp.bfloat16)
    by_column = lax.all_to_all(col_spec, ("row", "expert"), split_axis=3, concat_axis=2, tiled=True)
    modes = (product(forward_rows, by_column, "amch,gchkd->gamkd") * (1.0 / grid_len)).astype(
        jnp.bfloat16
    )
    mixed_modes = block_mlp(modes, spec_first, spec_second, spec_bias)
    row_back = product(inverse_rows, mixed_modes, "amch,gchkd->gamkd").astype(jnp.bfloat16)
    by_row = lax.all_to_all(row_back, ("row", "expert"), split_axis=2, concat_axis=3, tiled=True)
    mixing = product(by_row, inverse_cols, "gchkd,ckw->ghwd") * (1.0 / grid_len)
    residual = (tokens.astype(jnp.float32) + mixing).astype(jnp.bfloat16)
    normed = layer_norm(residual, ln_second).astype(jnp.bfloat16).reshape(-1, width)
    n_tokens = normed.shape[0]
    top_count = routing.shape[-1]
    experts = lax.axis_size("row") // 2
    capacity = n_tokens * top_count // experts
    flat_route = routing.reshape(-1)
    one_hot = (flat_route[:, None] == jnp.arange(experts, dtype=jnp.int32)[None, :]).astype(
        jnp.int32
    )
    earlier = jnp.cumsum(one_hot, axis=0) - one_hot
    slot_index = flat_route * capacity + jnp.sum(earlier * one_hot, axis=1)
    token_of = jnp.arange(n_tokens * top_count, dtype=jnp.int32) // top_count
    source_row = jnp.zeros((experts * capacity,), jnp.int32).at[slot_index].set(token_of)
    send_rows = normed[source_row].reshape(experts, capacity, width)
    partner_up, partner_down = from_partner((up_weight, down_weight), "row", 0)
    up_full = jnp.concatenate([up_weight[0], partner_up[0]], axis=1)
    down_full = jnp.concatenate([down_weight[0], partner_down[0]], axis=0)
    outgoing = send_rows.reshape(experts * 2, capacity // 2, width)
    returned = run_expert(
        lax.all_to_all(outgoing, "row", split_axis=0, concat_axis=0, tiled=True), up_full, down_full
    )
    results = returned.reshape(experts, capacity, width)
    gathered = results.reshape(-1, width)[slot_index].reshape(n_tokens, top_count, width)
    moe_out = jnp.sum(gathered * combine.reshape(n_tokens, top_count, 1), axis=1)
    final = residual.reshape(-1, width).astype(jnp.float32) + moe_out
    return final.reshape(tokens.shape).astype(jnp.bfloat16)


LANES = 256
PARTS = 4
EARLY_CHUNK = 3


def rank_tables(length, ranks):
    counter = np.arange(length)
    angle = 2.0 * np.pi / length * np.mod(np.outer(counter, counter), length)
    cosine, sine = np.cos(angle), np.sin(angle)
    half = length // 2
    second = -sine[:half]
    second[0] = cosine[half]
    packed = np.stack([cosine[:half], second])
    packed = packed.reshape(2, ranks, half // ranks, length).transpose(1, 0, 2, 3)
    packed = packed.reshape(length, length)
    tables = np.stack([cosine, sine, packed, packed.T])
    return jnp.asarray(tables, jnp.float32).astype(jnp.bfloat16)


def pick(index, values):
    out = values[-1]
    for place, value in enumerate(values[:-1]):
        out = jnp.where(index == place, value, out)
    return out


def norm_rows(values, gain):
    center = values - jnp.mean(values, axis=-1, keepdims=True)
    spread = jnp.mean(center * center, axis=-1, keepdims=True)
    return center * lax.rsqrt(spread + 1e-05) * gain


def block_kernel(
    sizes,
    tokens_ref,
    ln_first_ref,
    ln_second_ref,
    tables_ref,
    first_ref,
    second_ref,
    bias_ref,
    route_ref,
    weight_ref,
    up_hbm,
    down_hbm,
    out_ref,
    columns,
    rows_d,
    rows_dt,
    spec_send,
    spec_recv,
    back_send,
    back_recv,
    resid,
    acts,
    gates,
    total,
    ups,
    downs,
    a2a_send,
    a2a_recv,
    z_send,
    z_recv,
    x_send,
    x_recv,
    c_send,
    c_recv,
    swap_send,
    swap_recv,
    local_sem,
):
    groups, rows_axis, cores = sizes
    planes = rows_axis // 2
    ranks = rows_axis * cores
    group, row, core = lax.axis_index("group"), lax.axis_index("row"), lax.axis_index("expert")
    plane = row // 2
    me = row * cores + core
    n_tokens, width = tokens_ref.shape
    lanes = spec_send.shape[2]
    chunks = width // lanes
    grid_len = tables_ref.shape[1]
    slots = grid_len // 2 // ranks
    block_rows = n_tokens // ranks
    bwidth = first_ref.shape[2]
    per_step = lanes // bwidth
    scale = 1.0 / grid_len
    hidden = ups.shape[2]
    step = n_tokens // 2
    bf16 = jnp.bfloat16

    def device(g, r, c):
        return {"group": g, "row": r, "expert": c}

    def remote(source, target, send, recv, where):
        return pltpu.make_async_remote_copy(
            src_ref=source,
            dst_ref=target,
            send_sem=send,
            recv_sem=recv,
            device_id=where,
            device_id_type=pl.DeviceIdType.MESH,
        )

    barrier = pltpu.get_barrier_semaphore()
    for offset in range(1, ranks):
        other = lax.rem(me + offset, ranks)
        pl.semaphore_signal(
            barrier,
            inc=1,
            device_id=device(group, other // cores, other % cores),
            device_id_type=pl.DeviceIdType.MESH,
        )
    pl.semaphore_signal(
        barrier,
        inc=1,
        device_id=device(1 - group, row, core),
        device_id_type=pl.DeviceIdType.MESH,
    )

    @pl.loop(0, n_tokens // grid_len)
    def _(index):
        rows = pl.ds(pl.multiple_of(index * grid_len, grid_len), grid_len)
        acts[0, rows, :] = norm_rows(tokens_ref[rows, :].astype(jnp.float32), ln_first_ref[...]).astype(
            bf16
        )

    pl.semaphore_wait(barrier, ranks)

    shares = groups * cores
    share = group * cores + core
    side_share = (1 - group) * cores + core
    pieces = 2 * PARTS

    def view(ref, base, quarter, piece):
        size = ref.shape[1] // shares // PARTS
        start = (quarter * PARTS + piece % PARTS) * size
        return ref.at[base, pl.ds(pl.multiple_of(start, 32), size), :]

    def held(expert, quarter, piece):
        return view(ups if piece < PARTS else downs, expert, quarter, piece)

    def source(piece):
        return view(up_hbm if piece < PARTS else down_hbm, 0, share, piece)

    def plane_copy(expert, piece, src, way, target_plane):
        return remote(
            src,
            held(expert, share, piece),
            z_send.at[way, expert, piece],
            z_recv.at[expert, piece],
            device(group, 2 * target_plane + row % 2, core),
        )

    def side_copy(expert, piece):
        return remote(
            held(expert, share, piece),
            held(expert, share, piece),
            x_send.at[expert, piece],
            x_recv.at[expert, piece],
            device(1 - group, row, core),
        )

    def core_copy(expert, piece, which):
        part = held(expert, side_share if which else share, piece)
        return remote(
            part,
            part,
            c_send.at[which, expert, piece],
            c_recv.at[which, expert, piece],
            device(group, row, 1 - core),
        )

    near = plane + 1 - 2 * (plane % 2)
    far = plane - 1 + 2 * (plane % 2)
    inner = (far >= 0) & (far < planes)
    safe_far = jnp.clip(far, 0, planes - 1)
    arrivals = [[2 * (p // 2) + 1 - p % 2] for p in range(planes)]
    for p in range(planes):
        arrivals[p] += sorted((q for q in range(planes) if q // 2 != p // 2), key=lambda q: abs(q - p))
    expert_at = [plane] + [pick(plane, [a[t] for a in arrivals]) for t in range(planes - 1)]

    def own_copies(piece):
        return plane_copy(plane, piece, source(piece), 0, near)

    def far_own(piece):
        return plane_copy(plane, piece, source(piece), 1, safe_far)

    def forward(t, piece):
        expert = expert_at[t]
        target = safe_far if t == 1 else near
        return plane_copy(expert, piece, held(expert, share, piece), 0, target)

    def relay(t, piece, stage):
        expert = expert_at[t]
        if stage == 0:
            plane_copy(expert, piece, held(expert, share, piece), 0, near).wait_recv()
            if t > 1:

                @pl.when(inner)
                def _():
                    forward(t, piece).start()

            side_copy(expert, piece).start()
            core_copy(expert, piece, 0).start()
        else:
            side_copy(expert, piece).wait_recv()
            core_copy(expert, piece, 1).start()

    def ready(t):
        for piece in range(pieces):
            for which in range(2):
                core_copy(expert_at[t], piece, which).wait_recv()

    half = row % 2
    partner = device(group, row + 1 - 2 * half, core)
    gate_copy = remote(gates.at[0], gates.at[1], swap_send.at[0], swap_recv.at[0], partner)
    for piece in range(PARTS):
        own_copies(piece).start()

    early = pieces // 2

    @pl.when(inner)
    def _():
        for piece in range(early // 2):
            far_own(piece).start()

    up_local = pltpu.make_async_copy(up_hbm.at[0], ups.at[plane], local_sem.at[0])
    down_local = pltpu.make_async_copy(down_hbm.at[0], downs.at[plane], local_sem.at[1])
    up_local.start()
    down_local.start()

    my_rows = n_tokens // grid_len
    spread = jnp.broadcast_to(
        tables_ref[2].astype(jnp.float32)[:, None, :], (grid_len, my_rows, grid_len)
    ).reshape(n_tokens, grid_len)
    place = lax.broadcasted_iota(jnp.int32, (n_tokens, grid_len), 0) % my_rows
    for index in range(my_rows):
        columns[:, index * grid_len : (index + 1) * grid_len] = jnp.where(
            place == index, spread, 0.0
        ).astype(bf16)

    order = sorted(range(1, ranks), key=lambda offset: abs(offset - ranks // 2))

    def exchange(stage, send_ref, recv_ref, chunk, offset):
        other = lax.rem(me + offset, ranks)
        return remote(
            send_ref.at[chunk, pl.ds(pl.multiple_of(other * block_rows, block_rows), block_rows), :],
            recv_ref.at[chunk, pl.ds(pl.multiple_of(me * block_rows, block_rows), block_rows), :],
            a2a_send.at[stage, chunk, offset],
            a2a_recv.at[stage, chunk, offset],
            device(group, other // cores, other % cores),
        )

    def arrived(stage, send_ref, recv_ref, chunk, offset):
        other = lax.rem(me + ranks - offset, ranks)
        return remote(
            send_ref.at[chunk, pl.ds(pl.multiple_of(me * block_rows, block_rows), block_rows), :],
            recv_ref.at[chunk, pl.ds(pl.multiple_of(other * block_rows, block_rows), block_rows), :],
            a2a_send.at[stage, chunk, offset],
            a2a_recv.at[stage, chunk, offset],
            device(group, other // cores, other % cores),
        )

    def keep_own(send_ref, recv_ref, chunk):
        mine = pl.ds(pl.multiple_of(me * block_rows, block_rows), block_rows)
        recv_ref[chunk, mine, :] = send_ref[chunk, mine, :]

    @pl.loop(0, chunks)
    def _(chunk):
        cut = pl.ds(pl.multiple_of(chunk * lanes, lanes), lanes)
        spec_send[chunk] = jnp.dot(
            columns[...], acts[0, :, cut], preferred_element_type=jnp.float32
        ).astype(bf16)
        for offset in order:
            exchange(0, spec_send, spec_recv, chunk, offset).start()
        keep_own(spec_send, spec_recv, chunk)

    picker = lax.broadcasted_iota(jnp.int32, (grid_len, n_tokens), 1) // my_rows
    picker = picker == lax.broadcasted_iota(jnp.int32, (grid_len, n_tokens), 0)
    picker = jnp.where(picker, 1.0, 0.0).astype(bf16)
    spread_t = jnp.dot(tables_ref[3], picker, preferred_element_type=jnp.float32)
    place_t = lax.broadcasted_iota(jnp.int32, (grid_len, n_tokens), 1) % my_rows
    for index in range(my_rows):
        columns[index * grid_len : (index + 1) * grid_len, :] = jnp.where(
            place_t == index, spread_t, 0.0
        ).astype(bf16)
    cosine, sine = tables_ref[0], tables_ref[1]
    none = jnp.zeros_like(cosine)

    def fill(slot, grid):
        for index, (left, right) in enumerate(grid):
            cut = slice(index * grid_len, (index + 1) * grid_len)
            rows_d[slot, cut, :grid_len] = left
            rows_d[slot, cut, grid_len:] = right
            rows_dt[slot, :grid_len, cut] = left
            rows_dt[slot, grid_len:, cut] = right

    usual = [(cosine, sine), (cosine, -sine), (-sine, cosine), (-sine, -cosine)]
    fill(0, usual)

    @pl.when(me == 0)
    def _():
        fill(1, [(cosine, none), (none, cosine), (-sine, none), (none, -sine)])

    @pl.when(me != 0)
    def _():
        fill(1, usual)

    lane = lax.broadcasted_iota(jnp.int32, gates.shape[1:], 1)
    chosen = jnp.zeros(gates.shape[1:], jnp.float32)
    for k in range(route_ref.shape[1]):
        hit = route_ref[:, k : k + 1] == lane
        chosen = chosen + jnp.where(hit, weight_ref[:, k : k + 1], 0.0)
    gates[0] = chosen
    total[...] = jnp.zeros_like(total)

    def square(ref, block):
        real, imag = ref[0, block], ref[1, block]
        top = jnp.concatenate([real, imag], axis=1)
        return jnp.concatenate([top, jnp.concatenate([-imag, real], axis=1)], axis=0)

    def mix(chunk):
        values = spec_recv[chunk].astype(jnp.float32).reshape(ranks, 2 * slots, my_rows, lanes)
        real_parts, imag_parts = [], []
        for slot in range(slots):
            pair = jnp.concatenate(
                [
                    values[:, slot].reshape(grid_len, lanes),
                    values[:, slots + slot].reshape(grid_len, lanes),
                ],
                axis=0,
            ).astype(bf16)
            matrix = rows_d[1 if slot == 0 else 0]
            modes = jnp.dot(matrix, pair, preferred_element_type=jnp.float32) * scale
            modes = modes.astype(bf16)
            real_parts.append(modes[: 2 * grid_len])
            imag_parts.append(modes[2 * grid_len :])
        real = jnp.concatenate(real_parts, axis=0)
        imag = jnp.concatenate(imag_parts, axis=0)
        mixed_real, mixed_imag = [], []
        for index in range(per_step):
            block = chunk * per_step + index
            cut = slice(index * bwidth, (index + 1) * bwidth)
            both = jnp.concatenate([real[:, cut], imag[:, cut]], axis=1)
            place = pl.ds(pl.multiple_of(block * bwidth, bwidth), bwidth)
            bias = jnp.concatenate([bias_ref[0:1, place], bias_ref[1:2, place]], axis=1)
            hid = jnp.dot(both, square(first_ref, block), preferred_element_type=jnp.float32) + bias
            hid = jnp.maximum(hid, 0.0).astype(bf16)
            mixed = jnp.dot(hid, square(second_ref, block), preferred_element_type=jnp.float32)
            mixed = mixed.astype(bf16)
            mixed_real.append(mixed[:, :bwidth])
            mixed_imag.append(mixed[:, bwidth:])
        real = jnp.concatenate(mixed_real, axis=1)
        imag = jnp.concatenate(mixed_imag, axis=1)
        back_real, back_imag = [], []
        for slot in range(slots):
            cut = slice(slot * 2 * grid_len, (slot + 1) * 2 * grid_len)
            column = jnp.concatenate([real[cut], imag[cut]], axis=0)
            matrix = rows_dt[1 if slot == 0 else 0]
            back = jnp.dot(matrix, column, preferred_element_type=jnp.float32)
            back_real.append(back[:grid_len].reshape(ranks, my_rows, lanes))
            back_imag.append(back[grid_len:].reshape(ranks, my_rows, lanes))
        out = jnp.stack(back_real + back_imag, axis=1).reshape(n_tokens, lanes)
        back_send[chunk] = out.astype(bf16)

    @pl.loop(0, chunks)
    def _(chunk):
        @pl.when((chunk == EARLY_CHUNK) & inner)
        def _():
            for piece in range(early // 2):
                relay(2, piece, 0)

        for offset in order:
            arrived(0, spec_send, spec_recv, chunk, offset).wait_recv()
        mix(chunk)
        for offset in order:
            exchange(1, back_send, back_recv, chunk, offset).start()
        keep_own(back_send, back_recv, chunk)

        @pl.when(chunk == 0)
        def _():
            for piece in range(PARTS, pieces):
                own_copies(piece).start()
            gate_copy.start()

        @pl.when((chunk == 1) & inner)
        def _():
            for piece in range(early // 2, early):
                far_own(piece).start()

    for piece in range(PARTS):
        relay(1, piece, 0)

    @pl.when(inner)
    def _():
        for piece in range(early, pieces):
            far_own(piece).start()
        for piece in range(PARTS):
            forward(1, piece).start()

    @pl.loop(0, chunks)
    def _(chunk):
        @pl.when(chunk == 2)
        def _():
            for piece in range(PARTS):
                relay(1, piece, 1)
            for piece in range(PARTS, pieces):
                relay(1, piece, 0)

            @pl.when(inner)
            def _():
                for piece in range(PARTS, pieces):
                    forward(1, piece).start()
                for piece in range(early // 2, early):
                    relay(2, piece, 0)

        for offset in order:
            arrived(1, back_send, back_recv, chunk, offset).wait_recv()
        cut = pl.ds(pl.multiple_of(chunk * lanes, lanes), lanes)
        mixing = jnp.dot(columns[...], back_recv[chunk], preferred_element_type=jnp.float32) * scale
        resid[:, cut] = (tokens_ref[:, cut].astype(jnp.float32) + mixing).astype(bf16)

    def swap_copy(block):
        rows = pl.ds(block * step, step)
        return remote(
            acts.at[0, rows, :],
            acts.at[1, rows, :],
            swap_send.at[1 + block],
            swap_recv.at[1 + block],
            partner,
        )

    def return_copy(block):
        rows = pl.ds(pl.multiple_of(block * step, step), step)
        return remote(
            spec_send.at[:, rows, :],
            spec_recv.at[:, rows, :],
            swap_send.at[3 + block],
            swap_recv.at[3 + block],
            partner,
        )

    for block in range(2):

        @pl.loop(0, my_rows // 2)
        def _(index):
            start = block * step + index * grid_len
            rows = pl.ds(pl.multiple_of(start, grid_len), grid_len)
            acts[0, rows, :] = norm_rows(
                resid[rows, :].astype(jnp.float32), ln_second_ref[...]
            ).astype(bf16)

        swap_copy(block).start()

    @pl.loop(0, chunks)
    def _(chunk):
        for offset in order:
            exchange(0, spec_send, spec_recv, chunk, offset).wait_send()

    plan = [(0, 0, 0), (0, 1, 0), (0, 0, 1), (0, 1, 1)]
    plan += [(1, 0, 0), (1, 0, 1), (0, 0, 2), (0, 1, 2)]
    plan += [(1, 0, 2), (1, 1, 0), (1, 1, 1), (1, 1, 2)]
    plan += [(1, 0, 3), (1, 1, 3), (0, 0, 3), (0, 1, 3)]
    first_use = [plan.index((0, 0, t)) for t in range(3)] + [12]
    pace = 35.0 / pieces
    starts = {
        True: [0, 4, 9, 14, 24, 29, 34, 38, 43, 48, 52, 57, 61],
        False: [0, 5, 9, 14, 23, 28, 39, 44, 48, 53, 58, 62, 74],
    }

    def expected(t, piece, stage, inside):
        if inside:
            when = pace * (piece + 1 - early) if t == 2 else pace * (piece + 1 + early)
            return when + stage * (pace + 1.5)
        if stage == 0:
            return pace * piece + (-3 if t == 2 else 32)
        return pace * piece + (8 if t == 2 else 43)

    def schedule(inside):
        places = {}
        for t in (2, 3):
            for piece in range(pieces):
                for stage in range(2):
                    if inside and t == 2 and stage == 0 and piece < early:
                        continue
                    when = expected(t, piece, stage, inside)
                    place = next((k for k, start in enumerate(starts[inside]) if start >= when - 2), 12)
                    places.setdefault(min(place, first_use[t]), []).append((when, t, piece, stage))
        return places

    def lift(who, rows, expert, cut):
        return jnp.dot(
            acts[who, rows, :], ups[expert, :, cut], preferred_element_type=jnp.float32
        )

    @pl.loop(0, len(plan))
    def _(item):
        who = pick(item, [p[0] for p in plan])
        block = pick(item, [p[1] for p in plan])
        turn = pick(item, [p[2] for p in plan])

        @pl.when(item == 0)
        def _():
            up_local.wait()
            down_local.wait()

        @pl.when(item == first_use[1])
        def _():
            for piece in range(PARTS, pieces):
                relay(1, piece, 1)

        for inside in (True, False):

            @pl.when(inner if inside else jnp.logical_not(inner))
            def _():
                for place, passes in sorted(schedule(inside).items()):

                    @pl.when(item == place)
                    def _():
                        for _, t, piece, stage in sorted(passes):
                            relay(t, piece, stage)

        for t in range(1, planes):

            @pl.when(item == first_use[t])
            def _():
                ready(t)

        for index, place in ((0, 4), (1, 9)):

            @pl.when(item == place)
            def _():
                swap_copy(index).wait_recv()

        @pl.when(item == 4)
        def _():
            gate_copy.wait_recv()

        expert = pick(turn, expert_at)
        rows = pl.ds(pl.multiple_of(block * step, step), step)
        wide = 512 if hidden % 512 == 0 else hidden
        cuts = [pl.ds(start, wide) for start in range(0, hidden, wide)]
        out, ahead = None, lift(who, rows, expert, cuts[0])
        for index, cut in enumerate(cuts):
            raw = ahead
            if index + 1 < len(cuts):
                ahead = lift(who, rows, expert, cuts[index + 1])
            active = jax.nn.gelu(raw, approximate=True).astype(bf16)
            part = jnp.dot(active, downs[expert, cut, :], preferred_element_type=jnp.float32)
            out = part if out is None else out + part
        lane = lax.broadcasted_iota(jnp.int32, (step, gates.shape[2]), 1)
        gate = jnp.sum(jnp.where(lane == expert, gates[who, rows, :], 0.0), axis=1, keepdims=True)
        total[who, rows, :] = total[who, rows, :] + gate * out

        @pl.when((who == 1) & (turn == planes - 1))
        def _():
            for chunk in range(chunks):
                cut = slice(chunk * lanes, (chunk + 1) * lanes)
                spec_send[chunk, rows, :] = total[1, rows, cut].astype(bf16)
            return_copy(block).start()

    for block in range(2):
        return_copy(block).wait_recv()
        rows = pl.ds(block * step, step)
        for chunk in range(chunks):
            cut = slice(chunk * lanes, (chunk + 1) * lanes)
            final = resid[rows, cut].astype(jnp.float32) + total[0, rows, cut]
            final = final + spec_recv[chunk, rows, :].astype(jnp.float32)
            out_ref[rows, cut] = final.astype(bf16)

    for block in range(2):
        swap_copy(block).wait_send()
        return_copy(block).wait_send()
    gate_copy.wait_send()

    @pl.loop(0, chunks)
    def _(chunk):
        for offset in order:
            exchange(1, back_send, back_recv, chunk, offset).wait_send()

    for piece in range(pieces):
        own_copies(piece).wait_send()
        for t in range(1, planes):
            side_copy(expert_at[t], piece).wait_send()
            for which in range(2):
                core_copy(expert_at[t], piece, which).wait_send()

    @pl.when(inner)
    def _():
        for piece in range(pieces):
            far_own(piece).wait_send()
            for t in range(1, planes):
                forward(t, piece).wait_send()


def per_device_fused(
    sizes,
    tokens,
    ln_first,
    spec_first,
    spec_second,
    spec_bias,
    ln_second,
    routing,
    combine,
    up_weight,
    down_weight,
):
    groups, rows_axis, cores = sizes
    ranks, planes = rows_axis * cores, rows_axis // 2
    _, my_rows, grid_len, width = tokens.shape
    n_tokens = my_rows * grid_len
    lanes = LANES
    chunks = width // lanes
    route = routing.reshape(n_tokens, -1)
    weight = combine.reshape(n_tokens, -1)
    hidden = up_weight.shape[2]
    bf16 = jnp.bfloat16
    pieces = 2 * PARTS
    vmem = pl.BlockSpec(memory_space=pltpu.VMEM)
    hbm = pl.BlockSpec(memory_space=pl.ANY)
    dma = pltpu.SemaphoreType.DMA
    out = pl.pallas_call(
        lambda *refs: block_kernel(sizes, *refs),
        in_specs=[vmem] * 9 + [hbm] * 2,
        out_specs=vmem,
        out_shape=jax.ShapeDtypeStruct((n_tokens, width), bf16),
        scratch_shapes=[
            pltpu.VMEM((n_tokens, n_tokens), bf16),
            pltpu.VMEM((2, 4 * grid_len, 2 * grid_len), bf16),
            pltpu.VMEM((2, 2 * grid_len, 4 * grid_len), bf16),
            pltpu.VMEM((chunks, n_tokens, lanes), bf16),
            pltpu.VMEM((chunks, n_tokens, lanes), bf16),
            pltpu.VMEM((chunks, n_tokens, lanes), bf16),
            pltpu.VMEM((chunks, n_tokens, lanes), bf16),
            pltpu.VMEM((n_tokens, width), bf16),
            pltpu.VMEM((2, n_tokens, width), bf16),
            pltpu.VMEM((2, n_tokens, 128), jnp.float32),
            pltpu.VMEM((2, n_tokens, width), jnp.float32),
            pltpu.VMEM((planes,) + up_weight.shape[1:], bf16),
            pltpu.VMEM((planes,) + down_weight.shape[1:], bf16),
            dma((2, chunks, ranks)),
            dma((2, chunks, ranks)),
            dma((2, planes, pieces)),
            dma((planes, pieces)),
            dma((planes, pieces)),
            dma((planes, pieces)),
            dma((2, planes, pieces)),
            dma((2, planes, pieces)),
            dma((5,)),
            dma((5,)),
            dma((2,)),
        ],
        compiler_params=pltpu.CompilerParams(
            collective_id=0, has_side_effects=True, vmem_limit_bytes=67043328
        ),
        name="block",
    )(
        tokens.reshape(n_tokens, width),
        ln_first.reshape(1, width),
        ln_second.reshape(1, width),
        rank_tables(grid_len, ranks),
        spec_first,
        spec_second,
        spec_bias,
        route,
        weight,
        up_weight,
        down_weight,
    )
    return out.reshape(tokens.shape)


def solution(mesh):
    shape = mesh.shape
    group, row, expert = shape["group"], shape["row"], shape["expert"]
    cells = P("group", ("row", "expert"), None, None)
    weights = P("row", None, None)
    ins = (cells, P(), P(), P(), P(), P(), cells, cells, weights, weights)

    def run(*args):
        tokens, first, routing = args[0], args[2], args[6]
        ranks, planes = row * expert, row // 2
        fused = group == 2 and expert == 2 and planes == 4 and routing.shape[-1] == planes
        fused = fused and tokens.shape[0] == group and tokens.shape[1] == 8 * ranks
        fused = fused and (tokens.shape[2] // 2) % ranks == 0 and tokens.shape[2] == 128
        fused = fused and tokens.shape[3] % LANES == 0 and LANES % first.shape[2] == 0
        fused = fused and args[8].shape[1] % 256 == 0 and args[9].shape[1] % 256 == 0
        if fused:
            body = lambda *blocks: per_device_fused((group, row, expert), *blocks)
        else:
            body = per_device
        call = jax.shard_map(body, mesh=mesh, in_specs=ins, out_specs=cells, check_vma=False)
        return call(*args)

    return run
```

```python
import math

import jax
import jax.numpy as jnp
import numpy as np
from jax import lax
from jax.experimental import pallas as pl
from jax.experimental.pallas import tpu as pltpu
from jax.sharding import PartitionSpec as P


def from_partner(value, axis, stride):
    mask = 2**stride
    pairs = [(source, source ^ mask) for source in range(lax.axis_size(axis))]
    return lax.ppermute(value, axis, pairs)


def twiddle(length):
    counter = jnp.arange(length, dtype=jnp.float32)
    angle = 2.0 * math.pi / length * jnp.mod(jnp.outer(counter, counter), float(length))
    return (jnp.cos(angle), jnp.sin(angle))


def layer_norm(values, gain):
    values = values.astype(jnp.float32)
    center = values - jnp.mean(values, axis=-1, keepdims=True)
    spread = jnp.mean(center * center, axis=-1, keepdims=True)
    return center * lax.rsqrt(spread + 1e-05) * gain


def product(left, right, form):
    return jnp.einsum(form, left, right, preferred_element_type=jnp.float32)


def complex_blocks(real_in, imag_in, weight):
    form = "ghkbi,bio->ghkbo"
    real_out = product(real_in, weight[0], form) - product(imag_in, weight[1], form)
    imag_out = product(real_in, weight[1], form) + product(imag_in, weight[0], form)
    return (real_out, imag_out)


def block_mlp(modes, first, second, bias):
    dims = modes.shape
    nblocks = first.shape[1]
    bwidth = first.shape[2]
    real_part = modes[:, 0].reshape(dims[0], dims[2], dims[3], nblocks, bwidth)
    imag_part = modes[:, 1].reshape(dims[0], dims[2], dims[3], nblocks, bwidth)
    hid_real, hid_imag = complex_blocks(real_part, imag_part, first)
    hid_real = jax.nn.relu(hid_real + bias[0].reshape(nblocks, bwidth)).astype(jnp.bfloat16)
    hid_imag = jax.nn.relu(hid_imag + bias[1].reshape(nblocks, bwidth)).astype(jnp.bfloat16)
    out_real, out_imag = complex_blocks(hid_real, hid_imag, second)
    return jnp.stack([out_real, out_imag], axis=1).reshape(dims).astype(jnp.bfloat16)


def run_expert(arrived, up_full, down_full):
    in_shape = arrived.shape
    width = arrived.shape[2]
    hidden = jax.nn.gelu(
        jnp.dot(arrived.reshape(-1, width), up_full, preferred_element_type=jnp.float32),
        approximate=True,
    ).astype(jnp.bfloat16)
    partial_out = jnp.dot(hidden, down_full, preferred_element_type=jnp.float32).reshape(
        in_shape[0], in_shape[1], width
    )
    return lax.all_to_all(
        partial_out.astype(jnp.bfloat16), "row", split_axis=0, concat_axis=0, tiled=True
    ).astype(partial_out.dtype)


def per_device(
    tokens,
    ln_first,
    spec_first,
    spec_second,
    spec_bias,
    ln_second,
    routing,
    combine,
    up_weight,
    down_weight,
):
    grid_len = tokens.shape[2]
    width = tokens.shape[3]
    cosine, sine = twiddle(grid_len)
    forward_cols = jnp.stack([cosine, -sine], axis=1).astype(jnp.bfloat16)
    forward_rows = jnp.stack(
        [jnp.stack([cosine, sine], axis=1), jnp.stack([-sine, cosine], axis=1)], axis=0
    ).astype(jnp.bfloat16)
    inverse_rows = jnp.stack(
        [jnp.stack([cosine, -sine], axis=1), jnp.stack([sine, cosine], axis=1)], axis=0
    ).astype(jnp.bfloat16)
    inverse_cols = jnp.stack([cosine, -sine], axis=0).astype(jnp.bfloat16)
    normed_first = layer_norm(tokens, ln_first).astype(jnp.bfloat16)
    col_spec = product(normed_first, forward_cols, "ghwd,wck->gchkd").astype(jnp.bfloat16)
    by_column = lax.all_to_all(col_spec, ("row", "expert"), split_axis=3, concat_axis=2, tiled=True)
    modes = (product(forward_rows, by_column, "amch,gchkd->gamkd") * (1.0 / grid_len)).astype(
        jnp.bfloat16
    )
    mixed_modes = block_mlp(modes, spec_first, spec_second, spec_bias)
    row_back = product(inverse_rows, mixed_modes, "amch,gchkd->gamkd").astype(jnp.bfloat16)
    by_row = lax.all_to_all(row_back, ("row", "expert"), split_axis=2, concat_axis=3, tiled=True)
    mixing = product(by_row, inverse_cols, "gchkd,ckw->ghwd") * (1.0 / grid_len)
    residual = (tokens.astype(jnp.float32) + mixing).astype(jnp.bfloat16)
    normed = layer_norm(residual, ln_second).astype(jnp.bfloat16).reshape(-1, width)
    n_tokens = normed.shape[0]
    top_count = routing.shape[-1]
    experts = lax.axis_size("row") // 2
    capacity = n_tokens * top_count // experts
    flat_route = routing.reshape(-1)
    one_hot = (flat_route[:, None] == jnp.arange(experts, dtype=jnp.int32)[None, :]).astype(
        jnp.int32
    )
    earlier = jnp.cumsum(one_hot, axis=0) - one_hot
    slot_index = flat_route * capacity + jnp.sum(earlier * one_hot, axis=1)
    token_of = jnp.arange(n_tokens * top_count, dtype=jnp.int32) // top_count
    source_row = jnp.zeros((experts * capacity,), jnp.int32).at[slot_index].set(token_of)
    send_rows = normed[source_row].reshape(experts, capacity, width)
    partner_up, partner_down = from_partner((up_weight, down_weight), "row", 0)
    up_full = jnp.concatenate([up_weight[0], partner_up[0]], axis=1)
    down_full = jnp.concatenate([down_weight[0], partner_down[0]], axis=0)
    outgoing = send_rows.reshape(experts * 2, capacity // 2, width)
    returned = run_expert(
        lax.all_to_all(outgoing, "row", split_axis=0, concat_axis=0, tiled=True), up_full, down_full
    )
    results = returned.reshape(experts, capacity, width)
    gathered = results.reshape(-1, width)[slot_index].reshape(n_tokens, top_count, width)
    moe_out = jnp.sum(gathered * combine.reshape(n_tokens, top_count, 1), axis=1)
    final = residual.reshape(-1, width).astype(jnp.float32) + moe_out
    return final.reshape(tokens.shape).astype(jnp.bfloat16)


LANES = 256
PARTS = 4
EARLY_CHUNK = 3


def rank_tables(length, ranks):
    counter = np.arange(length)
    angle = 2.0 * np.pi / length * np.mod(np.outer(counter, counter), length)
    cosine, sine = np.cos(angle), np.sin(angle)
    half = length // 2
    second = -sine[:half]
    second[0] = cosine[half]
    packed = np.stack([cosine[:half], second])
    packed = packed.reshape(2, ranks, half // ranks, length).transpose(1, 0, 2, 3)
    packed = packed.reshape(length, length)
    tables = np.stack([cosine, sine, packed, packed.T])
    return jnp.asarray(tables, jnp.float32).astype(jnp.bfloat16)


def pick(index, values):
    out = values[-1]
    for place, value in enumerate(values[:-1]):
        out = jnp.where(index == place, value, out)
    return out


def norm_rows(values, gain):
    center = values - jnp.mean(values, axis=-1, keepdims=True)
    spread = jnp.mean(center * center, axis=-1, keepdims=True)
    return center * lax.rsqrt(spread + 1e-05) * gain


def block_kernel(
    sizes,
    tokens_ref,
    ln_first_ref,
    ln_second_ref,
    tables_ref,
    first_ref,
    second_ref,
    bias_ref,
    route_ref,
    weight_ref,
    up_hbm,
    down_hbm,
    out_ref,
    columns,
    rows_d,
    rows_dt,
    spec_send,
    spec_recv,
    back_send,
    back_recv,
    resid,
    acts,
    gates,
    total,
    ups,
    downs,
    a2a_send,
    a2a_recv,
    z_send,
    z_recv,
    x_send,
    x_recv,
    c_send,
    c_recv,
    swap_send,
    swap_recv,
    local_sem,
):
    groups, rows_axis, cores = sizes
    planes = rows_axis // 2
    ranks = rows_axis * cores
    group, row, core = lax.axis_index("group"), lax.axis_index("row"), lax.axis_index("expert")
    plane = row // 2
    me = row * cores + core
    n_tokens, width = tokens_ref.shape
    lanes = spec_send.shape[2]
    chunks = width // lanes
    grid_len = tables_ref.shape[1]
    slots = grid_len // 2 // ranks
    block_rows = n_tokens // ranks
    bwidth = first_ref.shape[2]
    per_step = lanes // bwidth
    scale = 1.0 / grid_len
    hidden = ups.shape[2]
    step = n_tokens // 2
    bf16 = jnp.bfloat16

    def device(g, r, c):
        return {"group": g, "row": r, "expert": c}

    def remote(source, target, send, recv, where):
        return pltpu.make_async_remote_copy(
            src_ref=source,
            dst_ref=target,
            send_sem=send,
            recv_sem=recv,
            device_id=where,
            device_id_type=pl.DeviceIdType.MESH,
        )

    barrier = pltpu.get_barrier_semaphore()
    for offset in range(1, ranks):
        other = lax.rem(me + offset, ranks)
        pl.semaphore_signal(
            barrier,
            inc=1,
            device_id=device(group, other // cores, other % cores),
            device_id_type=pl.DeviceIdType.MESH,
        )
    pl.semaphore_signal(
        barrier,
        inc=1,
        device_id=device(1 - group, row, core),
        device_id_type=pl.DeviceIdType.MESH,
    )

    @pl.loop(0, n_tokens // grid_len)
    def _(index):
        rows = pl.ds(pl.multiple_of(index * grid_len, grid_len), grid_len)
        acts[0, rows, :] = norm_rows(tokens_ref[rows, :].astype(jnp.float32), ln_first_ref[...]).astype(
            bf16
        )

    pl.semaphore_wait(barrier, ranks)

    shares = groups * cores
    share = group * cores + core
    side_share = (1 - group) * cores + core
    pieces = 2 * PARTS

    def view(ref, base, quarter, piece):
        size = ref.shape[1] // shares // PARTS
        start = (quarter * PARTS + piece % PARTS) * size
        return ref.at[base, pl.ds(pl.multiple_of(start, 32), size), :]

    def held(expert, quarter, piece):
        return view(ups if piece < PARTS else downs, expert, quarter, piece)

    def source(piece):
        return view(up_hbm if piece < PARTS else down_hbm, 0, share, piece)

    def plane_copy(expert, piece, src, way, target_plane):
        return remote(
            src,
            held(expert, share, piece),
            z_send.at[way, expert, piece],
            z_recv.at[expert, piece],
            device(group, 2 * target_plane + row % 2, core),
        )

    def side_copy(expert, piece):
        return remote(
            held(expert, share, piece),
            held(expert, share, piece),
            x_send.at[expert, piece],
            x_recv.at[expert, piece],
            device(1 - group, row, core),
        )

    def core_copy(expert, piece, which):
        part = held(expert, side_share if which else share, piece)
        return remote(
            part,
            part,
            c_send.at[which, expert, piece],
            c_recv.at[which, expert, piece],
            device(group, row, 1 - core),
        )

    near = plane + 1 - 2 * (plane % 2)
    far = plane - 1 + 2 * (plane % 2)
    inner = (far >= 0) & (far < planes)
    safe_far = jnp.clip(far, 0, planes - 1)
    arrivals = [[2 * (p // 2) + 1 - p % 2] for p in range(planes)]
    for p in range(planes):
        arrivals[p] += sorted((q for q in range(planes) if q // 2 != p // 2), key=lambda q: abs(q - p))
    expert_at = [plane] + [pick(plane, [a[t] for a in arrivals]) for t in range(planes - 1)]

    def own_copies(piece):
        return plane_copy(plane, piece, source(piece), 0, near)

    def far_own(piece):
        return plane_copy(plane, piece, source(piece), 1, safe_far)

    def forward(t, piece):
        expert = expert_at[t]
        target = safe_far if t == 1 else near
        return plane_copy(expert, piece, held(expert, share, piece), 0, target)

    def relay(t, piece, stage):
        expert = expert_at[t]
        if stage == 0:
            plane_copy(expert, piece, held(expert, share, piece), 0, near).wait_recv()
            if t > 1:

                @pl.when(inner)
                def _():
                    forward(t, piece).start()

            side_copy(expert, piece).start()
            core_copy(expert, piece, 0).start()
        else:
            side_copy(expert, piece).wait_recv()
            core_copy(expert, piece, 1).start()

    def ready(t):
        for piece in range(pieces):
            for which in range(2):
                core_copy(expert_at[t], piece, which).wait_recv()

    half = row % 2
    partner = device(group, row + 1 - 2 * half, core)
    gate_copy = remote(gates.at[0], gates.at[1], swap_send.at[0], swap_recv.at[0], partner)
    for piece in range(PARTS):
        own_copies(piece).start()

    early = pieces // 2

    @pl.when(inner)
    def _():
        for piece in range(early // 2):
            far_own(piece).start()

    up_local = pltpu.make_async_copy(up_hbm.at[0], ups.at[plane], local_sem.at[0])
    down_local = pltpu.make_async_copy(down_hbm.at[0], downs.at[plane], local_sem.at[1])
    up_local.start()
    down_local.start()

    my_rows = n_tokens // grid_len
    spread = jnp.broadcast_to(
        tables_ref[2].astype(jnp.float32)[:, None, :], (grid_len, my_rows, grid_len)
    ).reshape(n_tokens, grid_len)
    place = lax.broadcasted_iota(jnp.int32, (n_tokens, grid_len), 0) % my_rows
    for index in range(my_rows):
        columns[:, index * grid_len : (index + 1) * grid_len] = jnp.where(
            place == index, spread, 0.0
        ).astype(bf16)

    order = sorted(range(1, ranks), key=lambda offset: abs(offset - ranks // 2))

    def exchange(stage, send_ref, recv_ref, chunk, offset):
        other = lax.rem(me + offset, ranks)
        return remote(
            send_ref.at[chunk, pl.ds(pl.multiple_of(other * block_rows, block_rows), block_rows), :],
            recv_ref.at[chunk, pl.ds(pl.multiple_of(me * block_rows, block_rows), block_rows), :],
            a2a_send.at[stage, chunk, offset],
            a2a_recv.at[stage, chunk, offset],
            device(group, other // cores, other % cores),
        )

    def arrived(stage, send_ref, recv_ref, chunk, offset):
        other = lax.rem(me + ranks - offset, ranks)
        return remote(
            send_ref.at[chunk, pl.ds(pl.multiple_of(me * block_rows, block_rows), block_rows), :],
            recv_ref.at[chunk, pl.ds(pl.multiple_of(other * block_rows, block_rows), block_rows), :],
            a2a_send.at[stage, chunk, offset],
            a2a_recv.at[stage, chunk, offset],
            device(group, other // cores, other % cores),
        )

    def keep_own(send_ref, recv_ref, chunk):
        mine = pl.ds(pl.multiple_of(me * block_rows, block_rows), block_rows)
        recv_ref[chunk, mine, :] = send_ref[chunk, mine, :]

    @pl.loop(0, chunks)
    def _(chunk):
        cut = pl.ds(pl.multiple_of(chunk * lanes, lanes), lanes)
        spec_send[chunk] = jnp.dot(
            columns[...], acts[0, :, cut], preferred_element_type=jnp.float32
        ).astype(bf16)
        for offset in order:
            exchange(0, spec_send, spec_recv, chunk, offset).start()
        keep_own(spec_send, spec_recv, chunk)

    picker = lax.broadcasted_iota(jnp.int32, (grid_len, n_tokens), 1) // my_rows
    picker = picker == lax.broadcasted_iota(jnp.int32, (grid_len, n_tokens), 0)
    picker = jnp.where(picker, 1.0, 0.0).astype(bf16)
    spread_t = jnp.dot(tables_ref[3], picker, preferred_element_type=jnp.float32)
    place_t = lax.broadcasted_iota(jnp.int32, (grid_len, n_tokens), 1) % my_rows
    for index in range(my_rows):
        columns[index * grid_len : (index + 1) * grid_len, :] = jnp.where(
            place_t == index, spread_t, 0.0
        ).astype(bf16)
    cosine, sine = tables_ref[0], tables_ref[1]
    none = jnp.zeros_like(cosine)

    def fill(slot, grid):
        for index, (left, right) in enumerate(grid):
            cut = slice(index * grid_len, (index + 1) * grid_len)
            rows_d[slot, cut, :grid_len] = left
            rows_d[slot, cut, grid_len:] = right
            rows_dt[slot, :grid_len, cut] = left
            rows_dt[slot, grid_len:, cut] = right

    usual = [(cosine, sine), (cosine, -sine), (-sine, cosine), (-sine, -cosine)]
    fill(0, usual)

    @pl.when(me == 0)
    def _():
        fill(1, [(cosine, none), (none, cosine), (-sine, none), (none, -sine)])

    @pl.when(me != 0)
    def _():
        fill(1, usual)

    lane = lax.broadcasted_iota(jnp.int32, gates.shape[1:], 1)
    chosen = jnp.zeros(gates.shape[1:], jnp.float32)
    for k in range(route_ref.shape[1]):
        hit = route_ref[:, k : k + 1] == lane
        chosen = chosen + jnp.where(hit, weight_ref[:, k : k + 1], 0.0)
    gates[0] = chosen
    total[...] = jnp.zeros_like(total)

    def square(ref, block):
        real, imag = ref[0, block], ref[1, block]
        top = jnp.concatenate([real, imag], axis=1)
        return jnp.concatenate([top, jnp.concatenate([-imag, real], axis=1)], axis=0)

    def mix(chunk):
        values = spec_recv[chunk].astype(jnp.float32).reshape(ranks, 2 * slots, my_rows, lanes)
        real_parts, imag_parts = [], []
        for slot in range(slots):
            pair = jnp.concatenate(
                [
                    values[:, slot].reshape(grid_len, lanes),
                    values[:, slots + slot].reshape(grid_len, lanes),
                ],
                axis=0,
            ).astype(bf16)
            matrix = rows_d[1 if slot == 0 else 0]
            modes = jnp.dot(matrix, pair, preferred_element_type=jnp.float32) * scale
            modes = modes.astype(bf16)
            real_parts.append(modes[: 2 * grid_len])
            imag_parts.append(modes[2 * grid_len :])
        real = jnp.concatenate(real_parts, axis=0)
        imag = jnp.concatenate(imag_parts, axis=0)
        mixed_real, mixed_imag = [], []
        for index in range(per_step):
            block = chunk * per_step + index
            cut = slice(index * bwidth, (index + 1) * bwidth)
            both = jnp.concatenate([real[:, cut], imag[:, cut]], axis=1)
            place = pl.ds(pl.multiple_of(block * bwidth, bwidth), bwidth)
            bias = jnp.concatenate([bias_ref[0:1, place], bias_ref[1:2, place]], axis=1)
            hid = jnp.dot(both, square(first_ref, block), preferred_element_type=jnp.float32) + bias
            hid = jnp.maximum(hid, 0.0).astype(bf16)
            mixed = jnp.dot(hid, square(second_ref, block), preferred_element_type=jnp.float32)
            mixed = mixed.astype(bf16)
            mixed_real.append(mixed[:, :bwidth])
            mixed_imag.append(mixed[:, bwidth:])
        real = jnp.concatenate(mixed_real, axis=1)
        imag = jnp.concatenate(mixed_imag, axis=1)
        back_real, back_imag = [], []
        for slot in range(slots):
            cut = slice(slot * 2 * grid_len, (slot + 1) * 2 * grid_len)
            column = jnp.concatenate([real[cut], imag[cut]], axis=0)
            matrix = rows_dt[1 if slot == 0 else 0]
            back = jnp.dot(matrix, column, preferred_element_type=jnp.float32)
            back_real.append(back[:grid_len].reshape(ranks, my_rows, lanes))
            back_imag.append(back[grid_len:].reshape(ranks, my_rows, lanes))
        out = jnp.stack(back_real + back_imag, axis=1).reshape(n_tokens, lanes)
        back_send[chunk] = out.astype(bf16)

    @pl.loop(0, chunks)
    def _(chunk):
        @pl.when((chunk == EARLY_CHUNK) & inner)
        def _():
            for piece in range(early // 2):
                relay(2, piece, 0)

        for offset in order:
            arrived(0, spec_send, spec_recv, chunk, offset).wait_recv()
        mix(chunk)
        for offset in order:
            exchange(1, back_send, back_recv, chunk, offset).start()
        keep_own(back_send, back_recv, chunk)

        @pl.when(chunk == 0)
        def _():
            for piece in range(PARTS, pieces):
                own_copies(piece).start()
            gate_copy.start()

        @pl.when((chunk == 1) & inner)
        def _():
            for piece in range(early // 2, early):
                far_own(piece).start()

    for piece in range(PARTS):
        relay(1, piece, 0)

    @pl.when(inner)
    def _():
        for piece in range(early, pieces):
            far_own(piece).start()
        for piece in range(PARTS):
            forward(1, piece).start()

    @pl.loop(0, chunks)
    def _(chunk):
        @pl.when(chunk == 2)
        def _():
            for piece in range(PARTS):
                relay(1, piece, 1)
            for piece in range(PARTS, pieces):
                relay(1, piece, 0)

            @pl.when(inner)
            def _():
                for piece in range(PARTS, pieces):
                    forward(1, piece).start()
                for piece in range(early // 2, early):
                    relay(2, piece, 0)

        @pl.when((chunk == 3) & jnp.logical_not(inner))
        def _():
            for piece in range(early // 2):
                relay(2, piece, 0)

        for offset in order:
            arrived(1, back_send, back_recv, chunk, offset).wait_recv()
        cut = pl.ds(pl.multiple_of(chunk * lanes, lanes), lanes)
        mixing = jnp.dot(columns[...], back_recv[chunk], preferred_element_type=jnp.float32) * scale
        resid[:, cut] = (tokens_ref[:, cut].astype(jnp.float32) + mixing).astype(bf16)

    def swap_copy(block):
        rows = pl.ds(block * step, step)
        return remote(
            acts.at[0, rows, :],
            acts.at[1, rows, :],
            swap_send.at[1 + block],
            swap_recv.at[1 + block],
            partner,
        )

    def return_copy(block):
        rows = pl.ds(pl.multiple_of(block * step, step), step)
        return remote(
            spec_send.at[:, rows, :],
            spec_recv.at[:, rows, :],
            swap_send.at[3 + block],
            swap_recv.at[3 + block],
            partner,
        )

    for block in range(2):

        @pl.loop(0, my_rows // 2)
        def _(index):
            start = block * step + index * grid_len
            rows = pl.ds(pl.multiple_of(start, grid_len), grid_len)
            acts[0, rows, :] = norm_rows(
                resid[rows, :].astype(jnp.float32), ln_second_ref[...]
            ).astype(bf16)

        swap_copy(block).start()

    @pl.loop(0, chunks)
    def _(chunk):
        for offset in order:
            exchange(0, spec_send, spec_recv, chunk, offset).wait_send()

    plan = [(0, 0, 0), (0, 1, 0), (0, 0, 1), (0, 1, 1)]
    plan += [(1, 0, 0), (1, 0, 1), (0, 0, 2), (0, 1, 2)]
    plan += [(1, 0, 2), (1, 1, 0), (1, 1, 1), (1, 1, 2)]
    plan += [(1, 0, 3), (1, 1, 3), (0, 0, 3), (0, 1, 3)]
    first_use = [plan.index((0, 0, t)) for t in range(3)] + [12]
    pace = 35.0 / pieces
    starts = {
        True: [0, 4, 9, 14, 24, 29, 34, 38, 43, 48, 52, 57, 61],
        False: [0, 5, 9, 14, 23, 28, 39, 44, 48, 53, 58, 62, 74],
    }

    def expected(t, piece, stage, inside):
        if inside:
            when = pace * (piece + 1 - early) if t == 2 else pace * (piece + 1 + early)
            return when + stage * (pace + 1.5)
        if stage == 0:
            return pace * piece + (-3 if t == 2 else 32)
        return pace * piece + (3 if t == 2 else 39)

    def schedule(inside):
        places = {}
        for t in (2, 3):
            for piece in range(pieces):
                for stage in range(2):
                    if t == 2 and stage == 0 and piece < (early if inside else early // 2):
                        continue
                    when = expected(t, piece, stage, inside)
                    place = next((k for k, start in enumerate(starts[inside]) if start >= when - 2), 12)
                    places.setdefault(min(place, first_use[t]), []).append((when, t, piece, stage))
        return places

    def lift(who, rows, expert, cut):
        return jnp.dot(
            acts[who, rows, :], ups[expert, :, cut], preferred_element_type=jnp.float32
        )

    @pl.loop(0, len(plan))
    def _(item):
        who = pick(item, [p[0] for p in plan])
        block = pick(item, [p[1] for p in plan])
        turn = pick(item, [p[2] for p in plan])

        @pl.when(item == 0)
        def _():
            up_local.wait()
            down_local.wait()

        @pl.when(item == first_use[1])
        def _():
            for piece in range(PARTS, pieces):
                relay(1, piece, 1)

        for inside in (True, False):

            @pl.when(inner if inside else jnp.logical_not(inner))
            def _():
                for place, passes in sorted(schedule(inside).items()):

                    @pl.when(item == place)
                    def _():
                        for _, t, piece, stage in sorted(passes):
                            relay(t, piece, stage)

        for t in range(1, planes):

            @pl.when(item == first_use[t])
            def _():
                ready(t)

        for index, place in ((0, 4), (1, 9)):

            @pl.when(item == place)
            def _():
                swap_copy(index).wait_recv()

        @pl.when(item == 4)
        def _():
            gate_copy.wait_recv()

        expert = pick(turn, expert_at)
        rows = pl.ds(pl.multiple_of(block * step, step), step)
        wide = 512 if hidden % 512 == 0 else hidden
        cuts = [pl.ds(start, wide) for start in range(0, hidden, wide)]
        out, ahead = None, lift(who, rows, expert, cuts[0])
        for index, cut in enumerate(cuts):
            raw = ahead
            if index + 1 < len(cuts):
                ahead = lift(who, rows, expert, cuts[index + 1])
            active = jax.nn.gelu(raw, approximate=True).astype(bf16)
            part = jnp.dot(active, downs[expert, cut, :], preferred_element_type=jnp.float32)
            out = part if out is None else out + part
        lane = lax.broadcasted_iota(jnp.int32, (step, gates.shape[2]), 1)
        gate = jnp.sum(jnp.where(lane == expert, gates[who, rows, :], 0.0), axis=1, keepdims=True)
        total[who, rows, :] = total[who, rows, :] + gate * out

        @pl.when((who == 1) & (turn == planes - 1))
        def _():
            for chunk in range(chunks):
                cut = slice(chunk * lanes, (chunk + 1) * lanes)
                spec_send[chunk, rows, :] = total[1, rows, cut].astype(bf16)
            return_copy(block).start()

    for block in range(2):
        swap_copy(block).wait_send()
    gate_copy.wait_send()

    @pl.loop(0, chunks)
    def _(chunk):
        for offset in order:
            exchange(1, back_send, back_recv, chunk, offset).wait_send()

    for piece in range(pieces):
        own_copies(piece).wait_send()
        for t in range(1, planes):
            side_copy(expert_at[t], piece).wait_send()
            for which in range(2):
                core_copy(expert_at[t], piece, which).wait_send()

    @pl.when(inner)
    def _():
        for piece in range(pieces):
            far_own(piece).wait_send()
            for t in range(1, planes):
                forward(t, piece).wait_send()

    def out_copy(block):
        rows = pl.ds(block * step, step)
        return pltpu.make_async_copy(acts.at[0, rows, :], out_ref.at[rows, :], local_sem.at[2 + block])

    for block in range(2):
        return_copy(block).wait_recv()
        rows = pl.ds(block * step, step)
        for chunk in range(chunks):
            cut = slice(chunk * lanes, (chunk + 1) * lanes)
            final = resid[rows, cut].astype(jnp.float32) + total[0, rows, cut]
            final = final + spec_recv[chunk, rows, :].astype(jnp.float32)
            acts[0, rows, cut] = final.astype(bf16)
        out_copy(block).start()

    for block in range(2):
        return_copy(block).wait_send()
        out_copy(block).wait()


def per_device_fused(
    sizes,
    tokens,
    ln_first,
    spec_first,
    spec_second,
    spec_bias,
    ln_second,
    routing,
    combine,
    up_weight,
    down_weight,
):
    groups, rows_axis, cores = sizes
    ranks, planes = rows_axis * cores, rows_axis // 2
    _, my_rows, grid_len, width = tokens.shape
    n_tokens = my_rows * grid_len
    lanes = LANES
    chunks = width // lanes
    route = routing.reshape(n_tokens, -1)
    weight = combine.reshape(n_tokens, -1)
    hidden = up_weight.shape[2]
    bf16 = jnp.bfloat16
    pieces = 2 * PARTS
    vmem = pl.BlockSpec(memory_space=pltpu.VMEM)
    hbm = pl.BlockSpec(memory_space=pl.ANY)
    dma = pltpu.SemaphoreType.DMA
    out = pl.pallas_call(
        lambda *refs: block_kernel(sizes, *refs),
        in_specs=[vmem] * 9 + [hbm] * 2,
        out_specs=hbm,
        out_shape=jax.ShapeDtypeStruct((n_tokens, width), bf16),
        scratch_shapes=[
            pltpu.VMEM((n_tokens, n_tokens), bf16),
            pltpu.VMEM((2, 4 * grid_len, 2 * grid_len), bf16),
            pltpu.VMEM((2, 2 * grid_len, 4 * grid_len), bf16),
            pltpu.VMEM((chunks, n_tokens, lanes), bf16),
            pltpu.VMEM((chunks, n_tokens, lanes), bf16),
            pltpu.VMEM((chunks, n_tokens, lanes), bf16),
            pltpu.VMEM((chunks, n_tokens, lanes), bf16),
            pltpu.VMEM((n_tokens, width), bf16),
            pltpu.VMEM((2, n_tokens, width), bf16),
            pltpu.VMEM((2, n_tokens, 128), jnp.float32),
            pltpu.VMEM((2, n_tokens, width), jnp.float32),
            pltpu.VMEM((planes,) + up_weight.shape[1:], bf16),
            pltpu.VMEM((planes,) + down_weight.shape[1:], bf16),
            dma((2, chunks, ranks)),
            dma((2, chunks, ranks)),
            dma((2, planes, pieces)),
            dma((planes, pieces)),
            dma((planes, pieces)),
            dma((planes, pieces)),
            dma((2, planes, pieces)),
            dma((2, planes, pieces)),
            dma((5,)),
            dma((5,)),
            dma((4,)),
        ],
        compiler_params=pltpu.CompilerParams(
            collective_id=0, has_side_effects=True, vmem_limit_bytes=67043328
        ),
        name="block",
    )(
        tokens.reshape(n_tokens, width),
        ln_first.reshape(1, width),
        ln_second.reshape(1, width),
        rank_tables(grid_len, ranks),
        spec_first,
        spec_second,
        spec_bias,
        route,
        weight,
        up_weight,
        down_weight,
    )
    return out.reshape(tokens.shape)


def solution(mesh):
    shape = mesh.shape
    group, row, expert = shape["group"], shape["row"], shape["expert"]
    cells = P("group", ("row", "expert"), None, None)
    weights = P("row", None, None)
    ins = (cells, P(), P(), P(), P(), P(), cells, cells, weights, weights)

    def run(*args):
        tokens, first, routing = args[0], args[2], args[6]
        ranks, planes = row * expert, row // 2
        fused = group == 2 and expert == 2 and planes == 4 and routing.shape[-1] == planes
        fused = fused and tokens.shape[0] == group and tokens.shape[1] == 8 * ranks
        fused = fused and (tokens.shape[2] // 2) % ranks == 0 and tokens.shape[2] == 128
        fused = fused and tokens.shape[3] % LANES == 0 and LANES % first.shape[2] == 0
        fused = fused and args[8].shape[1] % 256 == 0 and args[9].shape[1] % 256 == 0
        if fused:
            body = lambda *blocks: per_device_fused((group, row, expert), *blocks)
        else:
            body = per_device
        call = jax.shard_map(body, mesh=mesh, in_specs=ins, out_specs=cells, check_vma=False)
        return call(*args)

    return run
```

```python
import math

import jax
import jax.numpy as jnp
import numpy as np
from jax import lax
from jax.experimental import pallas as pl
from jax.experimental.pallas import tpu as pltpu
from jax.sharding import PartitionSpec as P


def from_partner(value, axis, stride):
    mask = 2**stride
    pairs = [(source, source ^ mask) for source in range(lax.axis_size(axis))]
    return lax.ppermute(value, axis, pairs)


def twiddle(length):
    counter = jnp.arange(length, dtype=jnp.float32)
    angle = 2.0 * math.pi / length * jnp.mod(jnp.outer(counter, counter), float(length))
    return (jnp.cos(angle), jnp.sin(angle))


def layer_norm(values, gain):
    values = values.astype(jnp.float32)
    center = values - jnp.mean(values, axis=-1, keepdims=True)
    spread = jnp.mean(center * center, axis=-1, keepdims=True)
    return center * lax.rsqrt(spread + 1e-05) * gain


def product(left, right, form):
    return jnp.einsum(form, left, right, preferred_element_type=jnp.float32)


def complex_blocks(real_in, imag_in, weight):
    form = "ghkbi,bio->ghkbo"
    real_out = product(real_in, weight[0], form) - product(imag_in, weight[1], form)
    imag_out = product(real_in, weight[1], form) + product(imag_in, weight[0], form)
    return (real_out, imag_out)


def block_mlp(modes, first, second, bias):
    dims = modes.shape
    nblocks = first.shape[1]
    bwidth = first.shape[2]
    real_part = modes[:, 0].reshape(dims[0], dims[2], dims[3], nblocks, bwidth)
    imag_part = modes[:, 1].reshape(dims[0], dims[2], dims[3], nblocks, bwidth)
    hid_real, hid_imag = complex_blocks(real_part, imag_part, first)
    hid_real = jax.nn.relu(hid_real + bias[0].reshape(nblocks, bwidth)).astype(jnp.bfloat16)
    hid_imag = jax.nn.relu(hid_imag + bias[1].reshape(nblocks, bwidth)).astype(jnp.bfloat16)
    out_real, out_imag = complex_blocks(hid_real, hid_imag, second)
    return jnp.stack([out_real, out_imag], axis=1).reshape(dims).astype(jnp.bfloat16)


def run_expert(arrived, up_full, down_full):
    in_shape = arrived.shape
    width = arrived.shape[2]
    hidden = jax.nn.gelu(
        jnp.dot(arrived.reshape(-1, width), up_full, preferred_element_type=jnp.float32),
        approximate=True,
    ).astype(jnp.bfloat16)
    partial_out = jnp.dot(hidden, down_full, preferred_element_type=jnp.float32).reshape(
        in_shape[0], in_shape[1], width
    )
    return lax.all_to_all(
        partial_out.astype(jnp.bfloat16), "row", split_axis=0, concat_axis=0, tiled=True
    ).astype(partial_out.dtype)


def per_device(
    tokens,
    ln_first,
    spec_first,
    spec_second,
    spec_bias,
    ln_second,
    routing,
    combine,
    up_weight,
    down_weight,
):
    grid_len = tokens.shape[2]
    width = tokens.shape[3]
    cosine, sine = twiddle(grid_len)
    forward_cols = jnp.stack([cosine, -sine], axis=1).astype(jnp.bfloat16)
    forward_rows = jnp.stack(
        [jnp.stack([cosine, sine], axis=1), jnp.stack([-sine, cosine], axis=1)], axis=0
    ).astype(jnp.bfloat16)
    inverse_rows = jnp.stack(
        [jnp.stack([cosine, -sine], axis=1), jnp.stack([sine, cosine], axis=1)], axis=0
    ).astype(jnp.bfloat16)
    inverse_cols = jnp.stack([cosine, -sine], axis=0).astype(jnp.bfloat16)
    normed_first = layer_norm(tokens, ln_first).astype(jnp.bfloat16)
    col_spec = product(normed_first, forward_cols, "ghwd,wck->gchkd").astype(jnp.bfloat16)
    by_column = lax.all_to_all(col_spec, ("row", "expert"), split_axis=3, concat_axis=2, tiled=True)
    modes = (product(forward_rows, by_column, "amch,gchkd->gamkd") * (1.0 / grid_len)).astype(
        jnp.bfloat16
    )
    mixed_modes = block_mlp(modes, spec_first, spec_second, spec_bias)
    row_back = product(inverse_rows, mixed_modes, "amch,gchkd->gamkd").astype(jnp.bfloat16)
    by_row = lax.all_to_all(row_back, ("row", "expert"), split_axis=2, concat_axis=3, tiled=True)
    mixing = product(by_row, inverse_cols, "gchkd,ckw->ghwd") * (1.0 / grid_len)
    residual = (tokens.astype(jnp.float32) + mixing).astype(jnp.bfloat16)
    normed = layer_norm(residual, ln_second).astype(jnp.bfloat16).reshape(-1, width)
    n_tokens = normed.shape[0]
    top_count = routing.shape[-1]
    experts = lax.axis_size("row") // 2
    capacity = n_tokens * top_count // experts
    flat_route = routing.reshape(-1)
    one_hot = (flat_route[:, None] == jnp.arange(experts, dtype=jnp.int32)[None, :]).astype(
        jnp.int32
    )
    earlier = jnp.cumsum(one_hot, axis=0) - one_hot
    slot_index = flat_route * capacity + jnp.sum(earlier * one_hot, axis=1)
    token_of = jnp.arange(n_tokens * top_count, dtype=jnp.int32) // top_count
    source_row = jnp.zeros((experts * capacity,), jnp.int32).at[slot_index].set(token_of)
    send_rows = normed[source_row].reshape(experts, capacity, width)
    partner_up, partner_down = from_partner((up_weight, down_weight), "row", 0)
    up_full = jnp.concatenate([up_weight[0], partner_up[0]], axis=1)
    down_full = jnp.concatenate([down_weight[0], partner_down[0]], axis=0)
    outgoing = send_rows.reshape(experts * 2, capacity // 2, width)
    returned = run_expert(
        lax.all_to_all(outgoing, "row", split_axis=0, concat_axis=0, tiled=True), up_full, down_full
    )
    results = returned.reshape(experts, capacity, width)
    gathered = results.reshape(-1, width)[slot_index].reshape(n_tokens, top_count, width)
    moe_out = jnp.sum(gathered * combine.reshape(n_tokens, top_count, 1), axis=1)
    final = residual.reshape(-1, width).astype(jnp.float32) + moe_out
    return final.reshape(tokens.shape).astype(jnp.bfloat16)


LANES = 256
PARTS = 4
EARLY_CHUNK = 3


def rank_tables(length, ranks):
    counter = np.arange(length)
    angle = 2.0 * np.pi / length * np.mod(np.outer(counter, counter), length)
    cosine, sine = np.cos(angle), np.sin(angle)
    half = length // 2
    second = -sine[:half]
    second[0] = cosine[half]
    packed = np.stack([cosine[:half], second])
    packed = packed.reshape(2, ranks, half // ranks, length).transpose(1, 0, 2, 3)
    packed = packed.reshape(length, length)
    tables = np.stack([cosine, sine, packed, packed.T])
    return jnp.asarray(tables, jnp.float32).astype(jnp.bfloat16)


def pick(index, values):
    out = values[-1]
    for place, value in enumerate(values[:-1]):
        out = jnp.where(index == place, value, out)
    return out


def norm_rows(values, gain):
    center = values - jnp.mean(values, axis=-1, keepdims=True)
    spread = jnp.mean(center * center, axis=-1, keepdims=True)
    return center * lax.rsqrt(spread + 1e-05) * gain


def block_kernel(
    sizes,
    tokens_ref,
    ln_first_ref,
    ln_second_ref,
    tables_ref,
    first_ref,
    second_ref,
    bias_ref,
    route_ref,
    weight_ref,
    up_hbm,
    down_hbm,
    out_ref,
    columns,
    rows_d,
    rows_dt,
    spec_send,
    spec_recv,
    back_send,
    back_recv,
    resid,
    acts,
    gates,
    total,
    ups,
    downs,
    a2a_send,
    a2a_recv,
    z_send,
    z_recv,
    x_send,
    x_recv,
    c_send,
    c_recv,
    swap_send,
    swap_recv,
    local_sem,
):
    groups, rows_axis, cores = sizes
    planes = rows_axis // 2
    ranks = rows_axis * cores
    group, row, core = lax.axis_index("group"), lax.axis_index("row"), lax.axis_index("expert")
    plane = row // 2
    me = row * cores + core
    n_tokens, width = tokens_ref.shape
    lanes = spec_send.shape[2]
    chunks = width // lanes
    grid_len = tables_ref.shape[1]
    slots = grid_len // 2 // ranks
    block_rows = n_tokens // ranks
    bwidth = first_ref.shape[2]
    per_step = lanes // bwidth
    scale = 1.0 / grid_len
    hidden = ups.shape[2]
    step = n_tokens // 2
    bf16 = jnp.bfloat16

    def device(g, r, c):
        return {"group": g, "row": r, "expert": c}

    def remote(source, target, send, recv, where):
        return pltpu.make_async_remote_copy(
            src_ref=source,
            dst_ref=target,
            send_sem=send,
            recv_sem=recv,
            device_id=where,
            device_id_type=pl.DeviceIdType.MESH,
        )

    barrier = pltpu.get_barrier_semaphore()
    for offset in range(1, ranks):
        other = lax.rem(me + offset, ranks)
        pl.semaphore_signal(
            barrier,
            inc=1,
            device_id=device(group, other // cores, other % cores),
            device_id_type=pl.DeviceIdType.MESH,
        )
    pl.semaphore_signal(
        barrier,
        inc=1,
        device_id=device(1 - group, row, core),
        device_id_type=pl.DeviceIdType.MESH,
    )

    @pl.loop(0, n_tokens // grid_len)
    def _(index):
        rows = pl.ds(pl.multiple_of(index * grid_len, grid_len), grid_len)
        acts[0, rows, :] = norm_rows(tokens_ref[rows, :].astype(jnp.float32), ln_first_ref[...]).astype(
            bf16
        )

    pl.semaphore_wait(barrier, ranks)

    shares = groups * cores
    share = group * cores + core
    side_share = (1 - group) * cores + core
    pieces = 2 * PARTS

    def view(ref, base, quarter, piece):
        size = ref.shape[1] // shares // PARTS
        start = (quarter * PARTS + piece % PARTS) * size
        return ref.at[base, pl.ds(pl.multiple_of(start, 32), size), :]

    def held(expert, quarter, piece):
        return view(ups if piece < PARTS else downs, expert, quarter, piece)

    def source(piece):
        return view(up_hbm if piece < PARTS else down_hbm, 0, share, piece)

    def plane_copy(expert, piece, src, way, target_plane):
        return remote(
            src,
            held(expert, share, piece),
            z_send.at[way, expert, piece],
            z_recv.at[expert, piece],
            device(group, 2 * target_plane + row % 2, core),
        )

    def side_copy(expert, piece):
        return remote(
            held(expert, share, piece),
            held(expert, share, piece),
            x_send.at[expert, piece],
            x_recv.at[expert, piece],
            device(1 - group, row, core),
        )

    def core_copy(expert, piece, which):
        part = held(expert, side_share if which else share, piece)
        return remote(
            part,
            part,
            c_send.at[which, expert, piece],
            c_recv.at[which, expert, piece],
            device(group, row, 1 - core),
        )

    near = plane + 1 - 2 * (plane % 2)
    far = plane - 1 + 2 * (plane % 2)
    inner = (far >= 0) & (far < planes)
    safe_far = jnp.clip(far, 0, planes - 1)
    arrivals = [[2 * (p // 2) + 1 - p % 2] for p in range(planes)]
    for p in range(planes):
        arrivals[p] += sorted((q for q in range(planes) if q // 2 != p // 2), key=lambda q: abs(q - p))
    expert_at = [plane] + [pick(plane, [a[t] for a in arrivals]) for t in range(planes - 1)]

    def own_copies(piece):
        return plane_copy(plane, piece, source(piece), 0, near)

    def far_own(piece):
        return plane_copy(plane, piece, source(piece), 1, safe_far)

    def forward(t, piece):
        expert = expert_at[t]
        target = safe_far if t == 1 else near
        return plane_copy(expert, piece, held(expert, share, piece), 0, target)

    def relay(t, piece, stage):
        expert = expert_at[t]
        if stage == 0:
            plane_copy(expert, piece, held(expert, share, piece), 0, near).wait_recv()
            if t > 1:

                @pl.when(inner)
                def _():
                    forward(t, piece).start()

            side_copy(expert, piece).start()
            core_copy(expert, piece, 0).start()
        else:
            side_copy(expert, piece).wait_recv()
            core_copy(expert, piece, 1).start()

    def ready(t):
        for piece in range(pieces):
            for which in range(2):
                core_copy(expert_at[t], piece, which).wait_recv()

    half = row % 2
    partner = device(group, row + 1 - 2 * half, core)
    gate_copy = remote(gates.at[0], gates.at[1], swap_send.at[0], swap_recv.at[0], partner)
    for piece in range(PARTS):
        own_copies(piece).start()

    early = pieces // 2

    @pl.when(inner)
    def _():
        for piece in range(early // 2):
            far_own(piece).start()

    up_local = pltpu.make_async_copy(up_hbm.at[0], ups.at[plane], local_sem.at[0])
    down_local = pltpu.make_async_copy(down_hbm.at[0], downs.at[plane], local_sem.at[1])
    up_local.start()
    down_local.start()

    my_rows = n_tokens // grid_len
    spread = jnp.broadcast_to(
        tables_ref[2].astype(jnp.float32)[:, None, :], (grid_len, my_rows, grid_len)
    ).reshape(n_tokens, grid_len)
    place = lax.broadcasted_iota(jnp.int32, (n_tokens, grid_len), 0) % my_rows
    for index in range(my_rows):
        columns[:, index * grid_len : (index + 1) * grid_len] = jnp.where(
            place == index, spread, 0.0
        ).astype(bf16)

    order = sorted(range(1, ranks), key=lambda offset: abs(offset - ranks // 2))

    def exchange(stage, send_ref, recv_ref, chunk, offset):
        other = lax.rem(me + offset, ranks)
        return remote(
            send_ref.at[chunk, pl.ds(pl.multiple_of(other * block_rows, block_rows), block_rows), :],
            recv_ref.at[chunk, pl.ds(pl.multiple_of(me * block_rows, block_rows), block_rows), :],
            a2a_send.at[stage, chunk, offset],
            a2a_recv.at[stage, chunk, offset],
            device(group, other // cores, other % cores),
        )

    def arrived(stage, send_ref, recv_ref, chunk, offset):
        other = lax.rem(me + ranks - offset, ranks)
        return remote(
            send_ref.at[chunk, pl.ds(pl.multiple_of(me * block_rows, block_rows), block_rows), :],
            recv_ref.at[chunk, pl.ds(pl.multiple_of(other * block_rows, block_rows), block_rows), :],
            a2a_send.at[stage, chunk, offset],
            a2a_recv.at[stage, chunk, offset],
            device(group, other // cores, other % cores),
        )

    def keep_own(send_ref, recv_ref, chunk):
        mine = pl.ds(pl.multiple_of(me * block_rows, block_rows), block_rows)
        recv_ref[chunk, mine, :] = send_ref[chunk, mine, :]

    @pl.loop(0, chunks)
    def _(chunk):
        cut = pl.ds(pl.multiple_of(chunk * lanes, lanes), lanes)
        spec_send[chunk] = jnp.dot(
            columns[...], acts[0, :, cut], preferred_element_type=jnp.float32
        ).astype(bf16)
        for offset in order:
            exchange(0, spec_send, spec_recv, chunk, offset).start()
        keep_own(spec_send, spec_recv, chunk)

    picker = lax.broadcasted_iota(jnp.int32, (grid_len, n_tokens), 1) // my_rows
    picker = picker == lax.broadcasted_iota(jnp.int32, (grid_len, n_tokens), 0)
    picker = jnp.where(picker, 1.0, 0.0).astype(bf16)
    spread_t = jnp.dot(tables_ref[3], picker, preferred_element_type=jnp.float32)
    place_t = lax.broadcasted_iota(jnp.int32, (grid_len, n_tokens), 1) % my_rows
    for index in range(my_rows):
        columns[index * grid_len : (index + 1) * grid_len, :] = jnp.where(
            place_t == index, spread_t, 0.0
        ).astype(bf16)
    cosine, sine = tables_ref[0], tables_ref[1]
    none = jnp.zeros_like(cosine)

    def fill(slot, grid):
        for index, (left, right) in enumerate(grid):
            cut = slice(index * grid_len, (index + 1) * grid_len)
            rows_d[slot, cut, :grid_len] = left
            rows_d[slot, cut, grid_len:] = right
            rows_dt[slot, :grid_len, cut] = left
            rows_dt[slot, grid_len:, cut] = right

    usual = [(cosine, sine), (cosine, -sine), (-sine, cosine), (-sine, -cosine)]
    fill(0, usual)

    @pl.when(me == 0)
    def _():
        fill(1, [(cosine, none), (none, cosine), (-sine, none), (none, -sine)])

    @pl.when(me != 0)
    def _():
        fill(1, usual)

    lane = lax.broadcasted_iota(jnp.int32, gates.shape[1:], 1)
    chosen = jnp.zeros(gates.shape[1:], jnp.float32)
    for k in range(route_ref.shape[1]):
        hit = route_ref[:, k : k + 1] == lane
        chosen = chosen + jnp.where(hit, weight_ref[:, k : k + 1], 0.0)
    gates[0] = chosen
    total[...] = jnp.zeros_like(total)

    def square(ref, block):
        real, imag = ref[0, block], ref[1, block]
        top = jnp.concatenate([real, imag], axis=1)
        return jnp.concatenate([top, jnp.concatenate([-imag, real], axis=1)], axis=0)

    def mix(chunk):
        values = spec_recv[chunk].astype(jnp.float32).reshape(ranks, 2 * slots, my_rows, lanes)
        real_parts, imag_parts = [], []
        for slot in range(slots):
            pair = jnp.concatenate(
                [
                    values[:, slot].reshape(grid_len, lanes),
                    values[:, slots + slot].reshape(grid_len, lanes),
                ],
                axis=0,
            ).astype(bf16)
            matrix = rows_d[1 if slot == 0 else 0]
            modes = jnp.dot(matrix, pair, preferred_element_type=jnp.float32) * scale
            modes = modes.astype(bf16)
            real_parts.append(modes[: 2 * grid_len])
            imag_parts.append(modes[2 * grid_len :])
        real = jnp.concatenate(real_parts, axis=0)
        imag = jnp.concatenate(imag_parts, axis=0)
        mixed_real, mixed_imag = [], []
        for index in range(per_step):
            block = chunk * per_step + index
            cut = slice(index * bwidth, (index + 1) * bwidth)
            both = jnp.concatenate([real[:, cut], imag[:, cut]], axis=1)
            place = pl.ds(pl.multiple_of(block * bwidth, bwidth), bwidth)
            bias = jnp.concatenate([bias_ref[0:1, place], bias_ref[1:2, place]], axis=1)
            hid = jnp.dot(both, square(first_ref, block), preferred_element_type=jnp.float32) + bias
            hid = jnp.maximum(hid, 0.0).astype(bf16)
            mixed = jnp.dot(hid, square(second_ref, block), preferred_element_type=jnp.float32)
            mixed = mixed.astype(bf16)
            mixed_real.append(mixed[:, :bwidth])
            mixed_imag.append(mixed[:, bwidth:])
        real = jnp.concatenate(mixed_real, axis=1)
        imag = jnp.concatenate(mixed_imag, axis=1)
        back_real, back_imag = [], []
        for slot in range(slots):
            cut = slice(slot * 2 * grid_len, (slot + 1) * 2 * grid_len)
            column = jnp.concatenate([real[cut], imag[cut]], axis=0)
            matrix = rows_dt[1 if slot == 0 else 0]
            back = jnp.dot(matrix, column, preferred_element_type=jnp.float32)
            back_real.append(back[:grid_len].reshape(ranks, my_rows, lanes))
            back_imag.append(back[grid_len:].reshape(ranks, my_rows, lanes))
        out = jnp.stack(back_real + back_imag, axis=1).reshape(n_tokens, lanes)
        back_send[chunk] = out.astype(bf16)

    @pl.loop(0, chunks)
    def _(chunk):
        @pl.when((chunk == EARLY_CHUNK) & inner)
        def _():
            for piece in range(early // 2):
                relay(2, piece, 0)

        for offset in order:
            arrived(0, spec_send, spec_recv, chunk, offset).wait_recv()
        mix(chunk)
        for offset in order:
            exchange(1, back_send, back_recv, chunk, offset).start()
        keep_own(back_send, back_recv, chunk)

        @pl.when(chunk == 0)
        def _():
            for piece in range(PARTS, pieces):
                own_copies(piece).start()
            gate_copy.start()

        @pl.when((chunk == 1) & inner)
        def _():
            for piece in range(early // 2, early):
                far_own(piece).start()

    for piece in range(PARTS):
        relay(1, piece, 0)

    @pl.when(inner)
    def _():
        for piece in range(early, pieces):
            far_own(piece).start()
        for piece in range(PARTS):
            forward(1, piece).start()

    @pl.loop(0, chunks)
    def _(chunk):
        @pl.when(chunk == 2)
        def _():
            for piece in range(PARTS):
                relay(1, piece, 1)
            for piece in range(PARTS, pieces):
                relay(1, piece, 0)

            @pl.when(inner)
            def _():
                for piece in range(PARTS, pieces):
                    forward(1, piece).start()

        @pl.when((chunk == 1) & inner)
        def _():
            for piece in range(early // 2, early):
                relay(2, piece, 0)

        @pl.when((chunk == 3) & jnp.logical_not(inner))
        def _():
            for piece in range(early // 2):
                relay(2, piece, 0)

        for offset in order:
            arrived(1, back_send, back_recv, chunk, offset).wait_recv()
        cut = pl.ds(pl.multiple_of(chunk * lanes, lanes), lanes)
        mixing = jnp.dot(columns[...], back_recv[chunk], preferred_element_type=jnp.float32) * scale
        resid[:, cut] = (tokens_ref[:, cut].astype(jnp.float32) + mixing).astype(bf16)

    def swap_copy(block):
        rows = pl.ds(block * step, step)
        return remote(
            acts.at[0, rows, :],
            acts.at[1, rows, :],
            swap_send.at[1 + block],
            swap_recv.at[1 + block],
            partner,
        )

    def return_copy(block):
        rows = pl.ds(pl.multiple_of(block * step, step), step)
        return remote(
            spec_send.at[:, rows, :],
            spec_recv.at[:, rows, :],
            swap_send.at[3 + block],
            swap_recv.at[3 + block],
            partner,
        )

    for block in range(2):

        @pl.loop(0, my_rows // 2)
        def _(index):
            start = block * step + index * grid_len
            rows = pl.ds(pl.multiple_of(start, grid_len), grid_len)
            acts[0, rows, :] = norm_rows(
                resid[rows, :].astype(jnp.float32), ln_second_ref[...]
            ).astype(bf16)

        swap_copy(block).start()

    @pl.loop(0, chunks)
    def _(chunk):
        for offset in order:
            exchange(0, spec_send, spec_recv, chunk, offset).wait_send()

    plan = [(0, 0, 0), (0, 1, 0), (0, 0, 1), (0, 1, 1)]
    plan += [(1, 0, 0), (1, 0, 1), (0, 0, 2), (0, 1, 2)]
    plan += [(1, 0, 2), (1, 1, 0), (1, 1, 1), (1, 1, 2)]
    plan += [(1, 0, 3), (1, 1, 3), (0, 0, 3), (0, 1, 3)]
    first_use = [plan.index((0, 0, t)) for t in range(3)] + [12]
    pace = 35.0 / pieces
    starts = {
        True: [0, 4, 9, 14, 24, 29, 34, 38, 43, 48, 52, 57, 61],
        False: [0, 5, 9, 14, 23, 28, 39, 44, 48, 53, 58, 62, 74],
    }

    def expected(t, piece, stage, inside):
        if inside:
            when = pace * (piece + 1 - early) if t == 2 else pace * (piece + 1 + early)
            return when + stage * (pace + 1.5)
        if stage == 0:
            return pace * piece + (-3 if t == 2 else 32)
        return pace * piece + (3 if t == 2 else 39)

    def schedule(inside):
        places = {}
        for t in (2, 3):
            for piece in range(pieces):
                for stage in range(2):
                    if t == 2 and stage == 0 and piece < (early if inside else early // 2):
                        continue
                    when = expected(t, piece, stage, inside)
                    place = next((k for k, start in enumerate(starts[inside]) if start >= when - 2), 12)
                    places.setdefault(min(place, first_use[t]), []).append((when, t, piece, stage))
        return places

    def lift(who, rows, expert, cut):
        return jnp.dot(
            acts[who, rows, :], ups[expert, :, cut], preferred_element_type=jnp.float32
        )

    @pl.loop(0, len(plan))
    def _(item):
        who = pick(item, [p[0] for p in plan])
        block = pick(item, [p[1] for p in plan])
        turn = pick(item, [p[2] for p in plan])

        @pl.when(item == 0)
        def _():
            up_local.wait()
            down_local.wait()

        @pl.when(item == first_use[1])
        def _():
            for piece in range(PARTS, pieces):
                relay(1, piece, 1)

        for inside in (True, False):

            @pl.when(inner if inside else jnp.logical_not(inner))
            def _():
                for place, passes in sorted(schedule(inside).items()):

                    @pl.when(item == place)
                    def _():
                        for _, t, piece, stage in sorted(passes):
                            relay(t, piece, stage)

        for t in range(1, planes):

            @pl.when(item == first_use[t])
            def _():
                ready(t)

        for index, place in ((0, 4), (1, 9)):

            @pl.when(item == place)
            def _():
                swap_copy(index).wait_recv()

        @pl.when(item == 4)
        def _():
            gate_copy.wait_recv()

        expert = pick(turn, expert_at)
        rows = pl.ds(pl.multiple_of(block * step, step), step)
        wide = 512 if hidden % 512 == 0 else hidden
        cuts = [pl.ds(start, wide) for start in range(0, hidden, wide)]
        out, ahead = None, lift(who, rows, expert, cuts[0])
        for index, cut in enumerate(cuts):
            raw = ahead
            if index + 1 < len(cuts):
                ahead = lift(who, rows, expert, cuts[index + 1])
            active = jax.nn.gelu(raw, approximate=True).astype(bf16)
            part = jnp.dot(active, downs[expert, cut, :], preferred_element_type=jnp.float32)
            out = part if out is None else out + part
        lane = lax.broadcasted_iota(jnp.int32, (step, gates.shape[2]), 1)
        gate = jnp.sum(jnp.where(lane == expert, gates[who, rows, :], 0.0), axis=1, keepdims=True)
        total[who, rows, :] = total[who, rows, :] + gate * out

        @pl.when((who == 1) & (turn == planes - 1))
        def _():
            for chunk in range(chunks):
                cut = slice(chunk * lanes, (chunk + 1) * lanes)
                spec_send[chunk, rows, :] = total[1, rows, cut].astype(bf16)
            return_copy(block).start()

    for block in range(2):
        swap_copy(block).wait_send()
    gate_copy.wait_send()

    @pl.loop(0, chunks)
    def _(chunk):
        for offset in order:
            exchange(1, back_send, back_recv, chunk, offset).wait_send()

    for piece in range(pieces):
        own_copies(piece).wait_send()
        for t in range(1, planes):
            side_copy(expert_at[t], piece).wait_send()
            for which in range(2):
                core_copy(expert_at[t], piece, which).wait_send()

    @pl.when(inner)
    def _():
        for piece in range(pieces):
            far_own(piece).wait_send()
            for t in range(1, planes):
                forward(t, piece).wait_send()

    def out_copy(block):
        rows = pl.ds(block * step, step)
        return pltpu.make_async_copy(acts.at[0, rows, :], out_ref.at[rows, :], local_sem.at[2 + block])

    for block in range(2):
        return_copy(block).wait_recv()
        rows = pl.ds(block * step, step)
        for chunk in range(chunks):
            cut = slice(chunk * lanes, (chunk + 1) * lanes)
            final = resid[rows, cut].astype(jnp.float32) + total[0, rows, cut]
            final = final + spec_recv[chunk, rows, :].astype(jnp.float32)
            acts[0, rows, cut] = final.astype(bf16)
        out_copy(block).start()

    for block in range(2):
        return_copy(block).wait_send()
        out_copy(block).wait()


def per_device_fused(
    sizes,
    tokens,
    ln_first,
    spec_first,
    spec_second,
    spec_bias,
    ln_second,
    routing,
    combine,
    up_weight,
    down_weight,
):
    groups, rows_axis, cores = sizes
    ranks, planes = rows_axis * cores, rows_axis // 2
    _, my_rows, grid_len, width = tokens.shape
    n_tokens = my_rows * grid_len
    lanes = LANES
    chunks = width // lanes
    route = routing.reshape(n_tokens, -1)
    weight = combine.reshape(n_tokens, -1)
    hidden = up_weight.shape[2]
    bf16 = jnp.bfloat16
    pieces = 2 * PARTS
    vmem = pl.BlockSpec(memory_space=pltpu.VMEM)
    hbm = pl.BlockSpec(memory_space=pl.ANY)
    dma = pltpu.SemaphoreType.DMA
    out = pl.pallas_call(
        lambda *refs: block_kernel(sizes, *refs),
        in_specs=[vmem] * 9 + [hbm] * 2,
        out_specs=hbm,
        out_shape=jax.ShapeDtypeStruct((n_tokens, width), bf16),
        scratch_shapes=[
            pltpu.VMEM((n_tokens, n_tokens), bf16),
            pltpu.VMEM((2, 4 * grid_len, 2 * grid_len), bf16),
            pltpu.VMEM((2, 2 * grid_len, 4 * grid_len), bf16),
            pltpu.VMEM((chunks, n_tokens, lanes), bf16),
            pltpu.VMEM((chunks, n_tokens, lanes), bf16),
            pltpu.VMEM((chunks, n_tokens, lanes), bf16),
            pltpu.VMEM((chunks, n_tokens, lanes), bf16),
            pltpu.VMEM((n_tokens, width), bf16),
            pltpu.VMEM((2, n_tokens, width), bf16),
            pltpu.VMEM((2, n_tokens, 128), jnp.float32),
            pltpu.VMEM((2, n_tokens, width), jnp.float32),
            pltpu.VMEM((planes,) + up_weight.shape[1:], bf16),
            pltpu.VMEM((planes,) + down_weight.shape[1:], bf16),
            dma((2, chunks, ranks)),
            dma((2, chunks, ranks)),
            dma((2, planes, pieces)),
            dma((planes, pieces)),
            dma((planes, pieces)),
            dma((planes, pieces)),
            dma((2, planes, pieces)),
            dma((2, planes, pieces)),
            dma((5,)),
            dma((5,)),
            dma((4,)),
        ],
        compiler_params=pltpu.CompilerParams(
            collective_id=0, has_side_effects=True, vmem_limit_bytes=67043328
        ),
        name="block",
    )(
        tokens.reshape(n_tokens, width),
        ln_first.reshape(1, width),
        ln_second.reshape(1, width),
        rank_tables(grid_len, ranks),
        spec_first,
        spec_second,
        spec_bias,
        route,
        weight,
        up_weight,
        down_weight,
    )
    return out.reshape(tokens.shape)


def solution(mesh):
    shape = mesh.shape
    group, row, expert = shape["group"], shape["row"], shape["expert"]
    cells = P("group", ("row", "expert"), None, None)
    weights = P("row", None, None)
    ins = (cells, P(), P(), P(), P(), P(), cells, cells, weights, weights)

    def run(*args):
        tokens, first, routing = args[0], args[2], args[6]
        ranks, planes = row * expert, row // 2
        fused = group == 2 and expert == 2 and planes == 4 and routing.shape[-1] == planes
        fused = fused and tokens.shape[0] == group and tokens.shape[1] == 8 * ranks
        fused = fused and (tokens.shape[2] // 2) % ranks == 0 and tokens.shape[2] == 128
        fused = fused and tokens.shape[3] % LANES == 0 and LANES % first.shape[2] == 0
        fused = fused and args[8].shape[1] % 256 == 0 and args[9].shape[1] % 256 == 0
        if fused:
            body = lambda *blocks: per_device_fused((group, row, expert), *blocks)
        else:
            body = per_device
        call = jax.shard_map(body, mesh=mesh, in_specs=ins, out_specs=cells, check_vma=False)
        return call(*args)

    return run
```

```python
import math

import jax
import jax.numpy as jnp
import numpy as np
from jax import lax
from jax.experimental import pallas as pl
from jax.experimental.pallas import tpu as pltpu
from jax.sharding import PartitionSpec as P


def from_partner(value, axis, stride):
    mask = 2**stride
    pairs = [(source, source ^ mask) for source in range(lax.axis_size(axis))]
    return lax.ppermute(value, axis, pairs)


def twiddle(length):
    counter = jnp.arange(length, dtype=jnp.float32)
    angle = 2.0 * math.pi / length * jnp.mod(jnp.outer(counter, counter), float(length))
    return (jnp.cos(angle), jnp.sin(angle))


def layer_norm(values, gain):
    values = values.astype(jnp.float32)
    center = values - jnp.mean(values, axis=-1, keepdims=True)
    spread = jnp.mean(center * center, axis=-1, keepdims=True)
    return center * lax.rsqrt(spread + 1e-05) * gain


def product(left, right, form):
    return jnp.einsum(form, left, right, preferred_element_type=jnp.float32)


def complex_blocks(real_in, imag_in, weight):
    form = "ghkbi,bio->ghkbo"
    real_out = product(real_in, weight[0], form) - product(imag_in, weight[1], form)
    imag_out = product(real_in, weight[1], form) + product(imag_in, weight[0], form)
    return (real_out, imag_out)


def block_mlp(modes, first, second, bias):
    dims = modes.shape
    nblocks = first.shape[1]
    bwidth = first.shape[2]
    real_part = modes[:, 0].reshape(dims[0], dims[2], dims[3], nblocks, bwidth)
    imag_part = modes[:, 1].reshape(dims[0], dims[2], dims[3], nblocks, bwidth)
    hid_real, hid_imag = complex_blocks(real_part, imag_part, first)
    hid_real = jax.nn.relu(hid_real + bias[0].reshape(nblocks, bwidth)).astype(jnp.bfloat16)
    hid_imag = jax.nn.relu(hid_imag + bias[1].reshape(nblocks, bwidth)).astype(jnp.bfloat16)
    out_real, out_imag = complex_blocks(hid_real, hid_imag, second)
    return jnp.stack([out_real, out_imag], axis=1).reshape(dims).astype(jnp.bfloat16)


def run_expert(arrived, up_full, down_full):
    in_shape = arrived.shape
    width = arrived.shape[2]
    hidden = jax.nn.gelu(
        jnp.dot(arrived.reshape(-1, width), up_full, preferred_element_type=jnp.float32),
        approximate=True,
    ).astype(jnp.bfloat16)
    partial_out = jnp.dot(hidden, down_full, preferred_element_type=jnp.float32).reshape(
        in_shape[0], in_shape[1], width
    )
    return lax.all_to_all(
        partial_out.astype(jnp.bfloat16), "row", split_axis=0, concat_axis=0, tiled=True
    ).astype(partial_out.dtype)


def per_device(
    tokens,
    ln_first,
    spec_first,
    spec_second,
    spec_bias,
    ln_second,
    routing,
    combine,
    up_weight,
    down_weight,
):
    grid_len = tokens.shape[2]
    width = tokens.shape[3]
    cosine, sine = twiddle(grid_len)
    forward_cols = jnp.stack([cosine, -sine], axis=1).astype(jnp.bfloat16)
    forward_rows = jnp.stack(
        [jnp.stack([cosine, sine], axis=1), jnp.stack([-sine, cosine], axis=1)], axis=0
    ).astype(jnp.bfloat16)
    inverse_rows = jnp.stack(
        [jnp.stack([cosine, -sine], axis=1), jnp.stack([sine, cosine], axis=1)], axis=0
    ).astype(jnp.bfloat16)
    inverse_cols = jnp.stack([cosine, -sine], axis=0).astype(jnp.bfloat16)
    normed_first = layer_norm(tokens, ln_first).astype(jnp.bfloat16)
    col_spec = product(normed_first, forward_cols, "ghwd,wck->gchkd").astype(jnp.bfloat16)
    by_column = lax.all_to_all(col_spec, ("row", "expert"), split_axis=3, concat_axis=2, tiled=True)
    modes = (product(forward_rows, by_column, "amch,gchkd->gamkd") * (1.0 / grid_len)).astype(
        jnp.bfloat16
    )
    mixed_modes = block_mlp(modes, spec_first, spec_second, spec_bias)
    row_back = product(inverse_rows, mixed_modes, "amch,gchkd->gamkd").astype(jnp.bfloat16)
    by_row = lax.all_to_all(row_back, ("row", "expert"), split_axis=2, concat_axis=3, tiled=True)
    mixing = product(by_row, inverse_cols, "gchkd,ckw->ghwd") * (1.0 / grid_len)
    residual = (tokens.astype(jnp.float32) + mixing).astype(jnp.bfloat16)
    normed = layer_norm(residual, ln_second).astype(jnp.bfloat16).reshape(-1, width)
    n_tokens = normed.shape[0]
    top_count = routing.shape[-1]
    experts = lax.axis_size("row") // 2
    capacity = n_tokens * top_count // experts
    flat_route = routing.reshape(-1)
    one_hot = (flat_route[:, None] == jnp.arange(experts, dtype=jnp.int32)[None, :]).astype(
        jnp.int32
    )
    earlier = jnp.cumsum(one_hot, axis=0) - one_hot
    slot_index = flat_route * capacity + jnp.sum(earlier * one_hot, axis=1)
    token_of = jnp.arange(n_tokens * top_count, dtype=jnp.int32) // top_count
    source_row = jnp.zeros((experts * capacity,), jnp.int32).at[slot_index].set(token_of)
    send_rows = normed[source_row].reshape(experts, capacity, width)
    partner_up, partner_down = from_partner((up_weight, down_weight), "row", 0)
    up_full = jnp.concatenate([up_weight[0], partner_up[0]], axis=1)
    down_full = jnp.concatenate([down_weight[0], partner_down[0]], axis=0)
    outgoing = send_rows.reshape(experts * 2, capacity // 2, width)
    returned = run_expert(
        lax.all_to_all(outgoing, "row", split_axis=0, concat_axis=0, tiled=True), up_full, down_full
    )
    results = returned.reshape(experts, capacity, width)
    gathered = results.reshape(-1, width)[slot_index].reshape(n_tokens, top_count, width)
    moe_out = jnp.sum(gathered * combine.reshape(n_tokens, top_count, 1), axis=1)
    final = residual.reshape(-1, width).astype(jnp.float32) + moe_out
    return final.reshape(tokens.shape).astype(jnp.bfloat16)


LANES = 256
PARTS = 4
EARLY_CHUNK = 2


def rank_tables(length, ranks):
    counter = np.arange(length)
    angle = 2.0 * np.pi / length * np.mod(np.outer(counter, counter), length)
    cosine, sine = np.cos(angle), np.sin(angle)
    half = length // 2
    second = -sine[:half]
    second[0] = cosine[half]
    packed = np.stack([cosine[:half], second])
    packed = packed.reshape(2, ranks, half // ranks, length).transpose(1, 0, 2, 3)
    packed = packed.reshape(length, length)
    tables = np.stack([cosine, sine, packed, packed.T])
    return jnp.asarray(tables, jnp.float32).astype(jnp.bfloat16)


def pick(index, values):
    out = values[-1]
    for place, value in enumerate(values[:-1]):
        out = jnp.where(index == place, value, out)
    return out


def norm_rows(values, gain):
    center = values - jnp.mean(values, axis=-1, keepdims=True)
    spread = jnp.mean(center * center, axis=-1, keepdims=True)
    return center * lax.rsqrt(spread + 1e-05) * gain


def block_kernel(
    sizes,
    tokens_ref,
    ln_first_ref,
    ln_second_ref,
    tables_ref,
    first_ref,
    second_ref,
    bias_ref,
    route_ref,
    weight_ref,
    up_hbm,
    down_hbm,
    out_ref,
    columns,
    rows_d,
    rows_dt,
    spec_send,
    spec_recv,
    back_send,
    back_recv,
    resid,
    acts,
    gates,
    total,
    ups,
    downs,
    a2a_send,
    a2a_recv,
    z_send,
    z_recv,
    x_send,
    x_recv,
    c_send,
    c_recv,
    swap_send,
    swap_recv,
    local_sem,
):
    groups, rows_axis, cores = sizes
    planes = rows_axis // 2
    ranks = rows_axis * cores
    group, row, core = lax.axis_index("group"), lax.axis_index("row"), lax.axis_index("expert")
    plane = row // 2
    me = row * cores + core
    n_tokens, width = tokens_ref.shape
    lanes = spec_send.shape[2]
    chunks = width // lanes
    grid_len = tables_ref.shape[1]
    slots = grid_len // 2 // ranks
    block_rows = n_tokens // ranks
    bwidth = first_ref.shape[2]
    per_step = lanes // bwidth
    scale = 1.0 / grid_len
    hidden = ups.shape[2]
    step = n_tokens // 2
    bf16 = jnp.bfloat16

    def device(g, r, c):
        return {"group": g, "row": r, "expert": c}

    def remote(source, target, send, recv, where):
        return pltpu.make_async_remote_copy(
            src_ref=source,
            dst_ref=target,
            send_sem=send,
            recv_sem=recv,
            device_id=where,
            device_id_type=pl.DeviceIdType.MESH,
        )

    barrier = pltpu.get_barrier_semaphore()
    for offset in range(1, ranks):
        other = lax.rem(me + offset, ranks)
        pl.semaphore_signal(
            barrier,
            inc=1,
            device_id=device(group, other // cores, other % cores),
            device_id_type=pl.DeviceIdType.MESH,
        )
    pl.semaphore_signal(
        barrier,
        inc=1,
        device_id=device(1 - group, row, core),
        device_id_type=pl.DeviceIdType.MESH,
    )

    @pl.loop(0, n_tokens // grid_len)
    def _(index):
        rows = pl.ds(pl.multiple_of(index * grid_len, grid_len), grid_len)
        acts[0, rows, :] = norm_rows(tokens_ref[rows, :].astype(jnp.float32), ln_first_ref[...]).astype(
            bf16
        )

    pl.semaphore_wait(barrier, ranks)

    shares = groups * cores
    share = group * cores + core
    side_share = (1 - group) * cores + core
    pieces = 2 * PARTS

    def view(ref, base, quarter, piece):
        size = ref.shape[1] // shares // PARTS
        start = (quarter * PARTS + piece % PARTS) * size
        return ref.at[base, pl.ds(pl.multiple_of(start, 32), size), :]

    def held(expert, quarter, piece):
        return view(ups if piece < PARTS else downs, expert, quarter, piece)

    def source(piece):
        return view(up_hbm if piece < PARTS else down_hbm, 0, share, piece)

    def plane_copy(expert, piece, src, way, target_plane):
        return remote(
            src,
            held(expert, share, piece),
            z_send.at[way, expert, piece],
            z_recv.at[expert, piece],
            device(group, 2 * target_plane + row % 2, core),
        )

    def side_copy(expert, piece):
        return remote(
            held(expert, share, piece),
            held(expert, share, piece),
            x_send.at[expert, piece],
            x_recv.at[expert, piece],
            device(1 - group, row, core),
        )

    def core_copy(expert, piece, which):
        part = held(expert, side_share if which else share, piece)
        return remote(
            part,
            part,
            c_send.at[which, expert, piece],
            c_recv.at[which, expert, piece],
            device(group, row, 1 - core),
        )

    near = plane + 1 - 2 * (plane % 2)
    far = plane - 1 + 2 * (plane % 2)
    inner = (far >= 0) & (far < planes)
    safe_far = jnp.clip(far, 0, planes - 1)
    arrivals = [[2 * (p // 2) + 1 - p % 2] for p in range(planes)]
    for p in range(planes):
        arrivals[p] += sorted((q for q in range(planes) if q // 2 != p // 2), key=lambda q: abs(q - p))
    expert_at = [plane] + [pick(plane, [a[t] for a in arrivals]) for t in range(planes - 1)]

    def own_copies(piece):
        return plane_copy(plane, piece, source(piece), 0, near)

    def far_own(piece):
        return plane_copy(plane, piece, source(piece), 1, safe_far)

    def forward(t, piece):
        expert = expert_at[t]
        target = safe_far if t == 1 else near
        return plane_copy(expert, piece, held(expert, share, piece), 0, target)

    def relay(t, piece, stage):
        expert = expert_at[t]
        if stage == 0:
            plane_copy(expert, piece, held(expert, share, piece), 0, near).wait_recv()
            if t > 1:

                @pl.when(inner)
                def _():
                    forward(t, piece).start()

            side_copy(expert, piece).start()
            core_copy(expert, piece, 0).start()
        else:
            side_copy(expert, piece).wait_recv()
            core_copy(expert, piece, 1).start()

    def ready(t):
        for piece in range(pieces):
            for which in range(2):
                core_copy(expert_at[t], piece, which).wait_recv()

    half = row % 2
    partner = device(group, row + 1 - 2 * half, core)
    gate_copy = remote(gates.at[0], gates.at[1], swap_send.at[0], swap_recv.at[0], partner)
    for piece in range(PARTS):
        own_copies(piece).start()

    early = pieces // 2

    @pl.when(inner)
    def _():
        for piece in range(early // 2):
            far_own(piece).start()

    up_local = pltpu.make_async_copy(up_hbm.at[0], ups.at[plane], local_sem.at[0])
    down_local = pltpu.make_async_copy(down_hbm.at[0], downs.at[plane], local_sem.at[1])
    up_local.start()
    down_local.start()

    my_rows = n_tokens // grid_len
    spread = jnp.broadcast_to(
        tables_ref[2].astype(jnp.float32)[:, None, :], (grid_len, my_rows, grid_len)
    ).reshape(n_tokens, grid_len)
    place = lax.broadcasted_iota(jnp.int32, (n_tokens, grid_len), 0) % my_rows
    for index in range(my_rows):
        columns[:, index * grid_len : (index + 1) * grid_len] = jnp.where(
            place == index, spread, 0.0
        ).astype(bf16)

    order = sorted(range(1, ranks), key=lambda offset: abs(offset - ranks // 2))

    def exchange(stage, send_ref, recv_ref, chunk, offset):
        other = lax.rem(me + offset, ranks)
        return remote(
            send_ref.at[chunk, pl.ds(pl.multiple_of(other * block_rows, block_rows), block_rows), :],
            recv_ref.at[chunk, pl.ds(pl.multiple_of(me * block_rows, block_rows), block_rows), :],
            a2a_send.at[stage, chunk, offset],
            a2a_recv.at[stage, chunk, offset],
            device(group, other // cores, other % cores),
        )

    def arrived(stage, send_ref, recv_ref, chunk, offset):
        other = lax.rem(me + ranks - offset, ranks)
        return remote(
            send_ref.at[chunk, pl.ds(pl.multiple_of(me * block_rows, block_rows), block_rows), :],
            recv_ref.at[chunk, pl.ds(pl.multiple_of(other * block_rows, block_rows), block_rows), :],
            a2a_send.at[stage, chunk, offset],
            a2a_recv.at[stage, chunk, offset],
            device(group, other // cores, other % cores),
        )

    def keep_own(send_ref, recv_ref, chunk):
        mine = pl.ds(pl.multiple_of(me * block_rows, block_rows), block_rows)
        recv_ref[chunk, mine, :] = send_ref[chunk, mine, :]

    @pl.loop(0, chunks)
    def _(chunk):
        cut = pl.ds(pl.multiple_of(chunk * lanes, lanes), lanes)
        spec_send[chunk] = jnp.dot(
            columns[...], acts[0, :, cut], preferred_element_type=jnp.float32
        ).astype(bf16)
        for offset in order:
            exchange(0, spec_send, spec_recv, chunk, offset).start()
        keep_own(spec_send, spec_recv, chunk)

    picker = lax.broadcasted_iota(jnp.int32, (grid_len, n_tokens), 1) // my_rows
    picker = picker == lax.broadcasted_iota(jnp.int32, (grid_len, n_tokens), 0)
    picker = jnp.where(picker, 1.0, 0.0).astype(bf16)
    spread_t = jnp.dot(tables_ref[3], picker, preferred_element_type=jnp.float32)
    place_t = lax.broadcasted_iota(jnp.int32, (grid_len, n_tokens), 1) % my_rows
    for index in range(my_rows):
        columns[index * grid_len : (index + 1) * grid_len, :] = jnp.where(
            place_t == index, spread_t, 0.0
        ).astype(bf16)
    cosine, sine = tables_ref[0], tables_ref[1]
    none = jnp.zeros_like(cosine)

    def fill(slot, grid):
        for index, (left, right) in enumerate(grid):
            cut = slice(index * grid_len, (index + 1) * grid_len)
            rows_d[slot, cut, :grid_len] = left
            rows_d[slot, cut, grid_len:] = right
            rows_dt[slot, :grid_len, cut] = left
            rows_dt[slot, grid_len:, cut] = right

    usual = [(cosine, sine), (cosine, -sine), (-sine, cosine), (-sine, -cosine)]
    fill(0, usual)

    @pl.when(me == 0)
    def _():
        fill(1, [(cosine, none), (none, cosine), (-sine, none), (none, -sine)])

    @pl.when(me != 0)
    def _():
        fill(1, usual)

    lane = lax.broadcasted_iota(jnp.int32, gates.shape[1:], 1)
    chosen = jnp.zeros(gates.shape[1:], jnp.float32)
    for k in range(route_ref.shape[1]):
        hit = route_ref[:, k : k + 1] == lane
        chosen = chosen + jnp.where(hit, weight_ref[:, k : k + 1], 0.0)
    gates[0] = chosen
    total[...] = jnp.zeros_like(total)

    def square(ref, block):
        real, imag = ref[0, block], ref[1, block]
        top = jnp.concatenate([real, imag], axis=1)
        return jnp.concatenate([top, jnp.concatenate([-imag, real], axis=1)], axis=0)

    def mix(chunk):
        values = spec_recv[chunk].astype(jnp.float32).reshape(ranks, 2 * slots, my_rows, lanes)
        real_parts, imag_parts = [], []
        for slot in range(slots):
            pair = jnp.concatenate(
                [
                    values[:, slot].reshape(grid_len, lanes),
                    values[:, slots + slot].reshape(grid_len, lanes),
                ],
                axis=0,
            ).astype(bf16)
            matrix = rows_d[1 if slot == 0 else 0]
            modes = jnp.dot(matrix, pair, preferred_element_type=jnp.float32) * scale
            modes = modes.astype(bf16)
            real_parts.append(modes[: 2 * grid_len])
            imag_parts.append(modes[2 * grid_len :])
        real = jnp.concatenate(real_parts, axis=0)
        imag = jnp.concatenate(imag_parts, axis=0)
        mixed_real, mixed_imag = [], []
        for index in range(per_step):
            block = chunk * per_step + index
            cut = slice(index * bwidth, (index + 1) * bwidth)
            both = jnp.concatenate([real[:, cut], imag[:, cut]], axis=1)
            place = pl.ds(pl.multiple_of(block * bwidth, bwidth), bwidth)
            bias = jnp.concatenate([bias_ref[0:1, place], bias_ref[1:2, place]], axis=1)
            hid = jnp.dot(both, square(first_ref, block), preferred_element_type=jnp.float32) + bias
            hid = jnp.maximum(hid, 0.0).astype(bf16)
            mixed = jnp.dot(hid, square(second_ref, block), preferred_element_type=jnp.float32)
            mixed = mixed.astype(bf16)
            mixed_real.append(mixed[:, :bwidth])
            mixed_imag.append(mixed[:, bwidth:])
        real = jnp.concatenate(mixed_real, axis=1)
        imag = jnp.concatenate(mixed_imag, axis=1)
        back_real, back_imag = [], []
        for slot in range(slots):
            cut = slice(slot * 2 * grid_len, (slot + 1) * 2 * grid_len)
            column = jnp.concatenate([real[cut], imag[cut]], axis=0)
            matrix = rows_dt[1 if slot == 0 else 0]
            back = jnp.dot(matrix, column, preferred_element_type=jnp.float32)
            back_real.append(back[:grid_len].reshape(ranks, my_rows, lanes))
            back_imag.append(back[grid_len:].reshape(ranks, my_rows, lanes))
        out = jnp.stack(back_real + back_imag, axis=1).reshape(n_tokens, lanes)
        back_send[chunk] = out.astype(bf16)

    @pl.loop(0, chunks)
    def _(chunk):
        @pl.when((chunk == EARLY_CHUNK) & inner)
        def _():
            for piece in range(early // 2):
                relay(2, piece, 0)

        for offset in order:
            arrived(0, spec_send, spec_recv, chunk, offset).wait_recv()
        mix(chunk)
        for offset in order:
            exchange(1, back_send, back_recv, chunk, offset).start()
        keep_own(back_send, back_recv, chunk)

        @pl.when(chunk == 0)
        def _():
            for piece in range(PARTS, pieces):
                own_copies(piece).start()
            gate_copy.start()

        @pl.when((chunk == 1) & inner)
        def _():
            for piece in range(early // 2, early):
                far_own(piece).start()

    for piece in range(PARTS):
        relay(1, piece, 0)

    @pl.when(inner)
    def _():
        for piece in range(early, pieces):
            far_own(piece).start()
        for piece in range(PARTS):
            forward(1, piece).start()

    @pl.loop(0, chunks)
    def _(chunk):
        @pl.when(chunk == 2)
        def _():
            for piece in range(PARTS):
                relay(1, piece, 1)
            for piece in range(PARTS, pieces):
                relay(1, piece, 0)

            @pl.when(inner)
            def _():
                for piece in range(PARTS, pieces):
                    forward(1, piece).start()

        @pl.when((chunk == 1) & inner)
        def _():
            for piece in range(early // 2, early):
                relay(2, piece, 0)

        @pl.when((chunk == 3) & jnp.logical_not(inner))
        def _():
            for piece in range(early // 2):
                relay(2, piece, 0)

        for offset in order:
            arrived(1, back_send, back_recv, chunk, offset).wait_recv()
        cut = pl.ds(pl.multiple_of(chunk * lanes, lanes), lanes)
        mixing = jnp.dot(columns[...], back_recv[chunk], preferred_element_type=jnp.float32) * scale
        resid[:, cut] = (tokens_ref[:, cut].astype(jnp.float32) + mixing).astype(bf16)

    def swap_copy(block):
        rows = pl.ds(block * step, step)
        return remote(
            acts.at[0, rows, :],
            acts.at[1, rows, :],
            swap_send.at[1 + block],
            swap_recv.at[1 + block],
            partner,
        )

    def return_copy(block):
        rows = pl.ds(pl.multiple_of(block * step, step), step)
        return remote(
            spec_send.at[:, rows, :],
            spec_recv.at[:, rows, :],
            swap_send.at[3 + block],
            swap_recv.at[3 + block],
            partner,
        )

    for block in range(2):

        @pl.loop(0, my_rows // 2)
        def _(index):
            start = block * step + index * grid_len
            rows = pl.ds(pl.multiple_of(start, grid_len), grid_len)
            acts[0, rows, :] = norm_rows(
                resid[rows, :].astype(jnp.float32), ln_second_ref[...]
            ).astype(bf16)

        swap_copy(block).start()

    @pl.loop(0, chunks)
    def _(chunk):
        for offset in order:
            exchange(0, spec_send, spec_recv, chunk, offset).wait_send()

    plan = [(0, 0, 0), (0, 1, 0), (0, 0, 1), (0, 1, 1)]
    plan += [(1, 0, 0), (1, 0, 1), (0, 0, 2), (0, 1, 2)]
    plan += [(1, 0, 2), (1, 1, 0), (1, 1, 1), (1, 1, 2)]
    plan += [(1, 0, 3), (1, 1, 3), (0, 0, 3), (0, 1, 3)]
    first_use = [plan.index((0, 0, t)) for t in range(3)] + [12]
    pace = 35.0 / pieces
    starts = {
        True: [0, 4, 9, 14, 24, 29, 34, 38, 43, 48, 52, 57, 61],
        False: [0, 5, 9, 14, 23, 28, 39, 44, 48, 53, 58, 62, 74],
    }

    def expected(t, piece, stage, inside):
        if inside:
            when = pace * (piece + 1 - early) if t == 2 else pace * (piece + 1 + early)
            return when + stage * (pace + 1.5)
        if stage == 0:
            return pace * piece + (-3 if t == 2 else 32)
        return pace * piece + (3 if t == 2 else 39)

    def schedule(inside):
        places = {}
        for t in (2, 3):
            for piece in range(pieces):
                for stage in range(2):
                    if t == 2 and stage == 0 and piece < (early if inside else early // 2):
                        continue
                    when = expected(t, piece, stage, inside)
                    place = next((k for k, start in enumerate(starts[inside]) if start >= when - 2), 12)
                    places.setdefault(min(place, first_use[t]), []).append((when, t, piece, stage))
        return places

    def lift(who, rows, expert, cut):
        return jnp.dot(
            acts[who, rows, :], ups[expert, :, cut], preferred_element_type=jnp.float32
        )

    @pl.loop(0, len(plan))
    def _(item):
        who = pick(item, [p[0] for p in plan])
        block = pick(item, [p[1] for p in plan])
        turn = pick(item, [p[2] for p in plan])

        @pl.when(item == 0)
        def _():
            up_local.wait()
            down_local.wait()

        @pl.when(item == first_use[1])
        def _():
            for piece in range(PARTS, pieces):
                relay(1, piece, 1)

        for inside in (True, False):

            @pl.when(inner if inside else jnp.logical_not(inner))
            def _():
                for place, passes in sorted(schedule(inside).items()):

                    @pl.when(item == place)
                    def _():
                        for _, t, piece, stage in sorted(passes):
                            relay(t, piece, stage)

        for t in range(1, planes):

            @pl.when(item == first_use[t])
            def _():
                ready(t)

        for index, place in ((0, 4), (1, 9)):

            @pl.when(item == place)
            def _():
                swap_copy(index).wait_recv()

        @pl.when(item == 4)
        def _():
            gate_copy.wait_recv()

        expert = pick(turn, expert_at)
        rows = pl.ds(pl.multiple_of(block * step, step), step)
        wide = 512 if hidden % 512 == 0 else hidden
        cuts = [pl.ds(start, wide) for start in range(0, hidden, wide)]
        out, ahead = None, lift(who, rows, expert, cuts[0])
        for index, cut in enumerate(cuts):
            raw = ahead
            if index + 1 < len(cuts):
                ahead = lift(who, rows, expert, cuts[index + 1])
            active = jax.nn.gelu(raw, approximate=True).astype(bf16)
            part = jnp.dot(active, downs[expert, cut, :], preferred_element_type=jnp.float32)
            out = part if out is None else out + part
        lane = lax.broadcasted_iota(jnp.int32, (step, gates.shape[2]), 1)
        gate = jnp.sum(jnp.where(lane == expert, gates[who, rows, :], 0.0), axis=1, keepdims=True)
        total[who, rows, :] = total[who, rows, :] + gate * out

        @pl.when((who == 1) & (turn == planes - 1))
        def _():
            for chunk in range(chunks):
                cut = slice(chunk * lanes, (chunk + 1) * lanes)
                spec_send[chunk, rows, :] = total[1, rows, cut].astype(bf16)
            return_copy(block).start()

    for block in range(2):
        swap_copy(block).wait_send()
    gate_copy.wait_send()

    @pl.loop(0, chunks)
    def _(chunk):
        for offset in order:
            exchange(1, back_send, back_recv, chunk, offset).wait_send()

    for piece in range(pieces):
        own_copies(piece).wait_send()
        for t in range(1, planes):
            side_copy(expert_at[t], piece).wait_send()
            for which in range(2):
                core_copy(expert_at[t], piece, which).wait_send()

    @pl.when(inner)
    def _():
        for piece in range(pieces):
            far_own(piece).wait_send()
            for t in range(1, planes):
                forward(t, piece).wait_send()

    def out_copy(block):
        rows = pl.ds(block * step, step)
        return pltpu.make_async_copy(acts.at[0, rows, :], out_ref.at[rows, :], local_sem.at[2 + block])

    for block in range(2):
        return_copy(block).wait_recv()
        rows = pl.ds(block * step, step)
        for chunk in range(chunks):
            cut = slice(chunk * lanes, (chunk + 1) * lanes)
            final = resid[rows, cut].astype(jnp.float32) + total[0, rows, cut]
            final = final + spec_recv[chunk, rows, :].astype(jnp.float32)
            acts[0, rows, cut] = final.astype(bf16)
        out_copy(block).start()

    for block in range(2):
        return_copy(block).wait_send()
        out_copy(block).wait()


def per_device_fused(
    sizes,
    tokens,
    ln_first,
    spec_first,
    spec_second,
    spec_bias,
    ln_second,
    routing,
    combine,
    up_weight,
    down_weight,
):
    groups, rows_axis, cores = sizes
    ranks, planes = rows_axis * cores, rows_axis // 2
    _, my_rows, grid_len, width = tokens.shape
    n_tokens = my_rows * grid_len
    lanes = LANES
    chunks = width // lanes
    route = routing.reshape(n_tokens, -1)
    weight = combine.reshape(n_tokens, -1)
    hidden = up_weight.shape[2]
    bf16 = jnp.bfloat16
    pieces = 2 * PARTS
    vmem = pl.BlockSpec(memory_space=pltpu.VMEM)
    hbm = pl.BlockSpec(memory_space=pl.ANY)
    dma = pltpu.SemaphoreType.DMA
    out = pl.pallas_call(
        lambda *refs: block_kernel(sizes, *refs),
        in_specs=[vmem] * 9 + [hbm] * 2,
        out_specs=hbm,
        out_shape=jax.ShapeDtypeStruct((n_tokens, width), bf16),
        scratch_shapes=[
            pltpu.VMEM((n_tokens, n_tokens), bf16),
            pltpu.VMEM((2, 4 * grid_len, 2 * grid_len), bf16),
            pltpu.VMEM((2, 2 * grid_len, 4 * grid_len), bf16),
            pltpu.VMEM((chunks, n_tokens, lanes), bf16),
            pltpu.VMEM((chunks, n_tokens, lanes), bf16),
            pltpu.VMEM((chunks, n_tokens, lanes), bf16),
            pltpu.VMEM((chunks, n_tokens, lanes), bf16),
            pltpu.VMEM((n_tokens, width), bf16),
            pltpu.VMEM((2, n_tokens, width), bf16),
            pltpu.VMEM((2, n_tokens, 128), jnp.float32),
            pltpu.VMEM((2, n_tokens, width), jnp.float32),
            pltpu.VMEM((planes,) + up_weight.shape[1:], bf16),
            pltpu.VMEM((planes,) + down_weight.shape[1:], bf16),
            dma((2, chunks, ranks)),
            dma((2, chunks, ranks)),
            dma((2, planes, pieces)),
            dma((planes, pieces)),
            dma((planes, pieces)),
            dma((planes, pieces)),
            dma((2, planes, pieces)),
            dma((2, planes, pieces)),
            dma((5,)),
            dma((5,)),
            dma((4,)),
        ],
        compiler_params=pltpu.CompilerParams(
            collective_id=0, has_side_effects=True, vmem_limit_bytes=67043328
        ),
        name="block",
    )(
        tokens.reshape(n_tokens, width),
        ln_first.reshape(1, width),
        ln_second.reshape(1, width),
        rank_tables(grid_len, ranks),
        spec_first,
        spec_second,
        spec_bias,
        route,
        weight,
        up_weight,
        down_weight,
    )
    return out.reshape(tokens.shape)


def solution(mesh):
    shape = mesh.shape
    group, row, expert = shape["group"], shape["row"], shape["expert"]
    cells = P("group", ("row", "expert"), None, None)
    weights = P("row", None, None)
    ins = (cells, P(), P(), P(), P(), P(), cells, cells, weights, weights)

    def run(*args):
        tokens, first, routing = args[0], args[2], args[6]
        ranks, planes = row * expert, row // 2
        fused = group == 2 and expert == 2 and planes == 4 and routing.shape[-1] == planes
        fused = fused and tokens.shape[0] == group and tokens.shape[1] == 8 * ranks
        fused = fused and (tokens.shape[2] // 2) % ranks == 0 and tokens.shape[2] == 128
        fused = fused and tokens.shape[3] % LANES == 0 and LANES % first.shape[2] == 0
        fused = fused and args[8].shape[1] % 256 == 0 and args[9].shape[1] % 256 == 0
        if fused:
            body = lambda *blocks: per_device_fused((group, row, expert), *blocks)
        else:
            body = per_device
        call = jax.shard_map(body, mesh=mesh, in_specs=ins, out_specs=cells, check_vma=False)
        return call(*args)

    return run
```
